32 devices in a mesh: groups: 2 (over y), seq: 16 (over z, x, core).
Axes of the slice: x: 2, y: 2, z: 4, core: 2. Of those that a mesh axis runs over, the one named last changes fastest.
Arguments:
- qkv: bfloat16 [4096, 32, 384], P(('groups', 'seq')), parts along dimension 0
- routes: int32 [4096, 32], P(('groups', 'seq')), parts along dimension 0, may hold values from 0 to 1, as said below
Outputs:
- attended: bfloat16 [4096, 32, 128], P(('groups', 'seq')), parts along dimension 0
The draws below stay inside these ranges and needn't reach their ends.
There are 2 independent parts, one for each index of `groups`. The reference program is written for one: setup_inputs(seed, part) draws one part's arguments, and reference() takes and returns one part's arrays. A program takes and returns all parts, laid end to end along the dimension named above; each array names one. Nothing has to cross between parts.
Inputs may be any that keep to these rules, and one draw needn't show every extreme that they name: Every cluster of every head holds between 512 and 1536 tokens, and in every head some cluster holds exactly 1536. Numbering the pairs (head h, cluster c) as h * 2 + c, the tokens of one device name each aligned group of 4 pairs exactly 256 times. Integer counts, offsets and slot indices derived from routes may cross between devices packed several to a 32-bit word.
All inputs are finite; a program needn't handle non-finite values.
Results may differ from the reference program's by a relative error of at most 0.0047.
Values may be sent and summed in bfloat16 or wider, within the bound.
No kernel may reach another device: no remote copies, remote signals or barrier semaphores. Data moves between devices by JAX's collectives and lax.ppermute only.
A program may use at most 128 MiB of HBM per device.

```python
import jax
import jax.numpy as jnp
from jax import lax

H = 32
DH = 128
TOK_DEV = 128
CLEN = 1024
TOKENS = 2048


def draw_routes(key, part):
    ndev = TOKENS // TOK_DEV
    kc = TOKENS // CLEN
    half = kc // 2
    share = CLEN // ndev
    amp = share // 2
    wobble = share // 4
    key_r, key_p, key_z, key_m = jax.random.split(key, 4)
    offsets = jax.random.randint(key_r, (H, half), -amp, amp + 1)
    chosen = jax.random.randint(key_p, (H,), 0, half)
    offsets = jnp.where(jnp.arange(half)[None, :] == chosen[:, None], amp, offsets)
    noise = jax.random.randint(key_z, (ndev, H, half), 0, wobble + 1)
    shifts = offsets[None] + noise - jnp.roll(noise, -1, axis=0)
    sizes = jnp.stack([share + shifts, share - shifts], axis=-1).reshape(ndev * H, kc)
    bounds = jnp.cumsum(sizes, axis=-1)
    ranks = jnp.arange(TOK_DEV, dtype=jnp.int32)
    labels = jax.vmap(lambda edge: jnp.searchsorted(edge, ranks, side='right'))(bounds).astype(jnp.int32)
    orders = jax.vmap(lambda sub: jax.random.permutation(sub, TOK_DEV))(jax.random.split(key_m, ndev * H))
    lines = jnp.arange(ndev * H, dtype=jnp.int32)[:, None]
    placed = jnp.zeros((ndev * H, TOK_DEV), jnp.int32).at[lines, orders].set(labels)
    placed = placed.reshape(ndev, H, TOK_DEV)
    return jnp.transpose(placed, (0, 2, 1)).reshape(TOKENS, H)


def draw_qkv(key, part):
    key_a = jax.random.fold_in(key, 0)
    shape = (TOKENS, H, 3 * DH)
    base = jnp.clip(jax.random.normal(key_a, shape, jnp.float32), -6.0, 6.0)
    return base.astype(jnp.bfloat16)


def setup_inputs(seed: int = 0, part: int = 0) -> dict:
    streams_of = jax.random.split(jax.random.key(seed), 3)
    part_splits = jax.random.split(jax.random.fold_in(streams_of[2], part), 3)
    return {
        "qkv": draw_qkv(jax.random.fold_in(jax.random.fold_in(streams_of[2], part), 71), part),
        "routes": draw_routes(jax.random.fold_in(jax.random.fold_in(streams_of[2], part), 71), part),
    }


def reference(qkv, routes):
    tokens, heads, width = qkv.shape
    head_size = width // 3
    clusters = tokens // CLEN
    capacity = 3 * CLEN // 2
    block_rows = CLEN // 2
    scale = 1.0 / (head_size ** 0.5)
    position = jnp.arange(tokens, dtype=jnp.int32)

    def one_cluster(tile):
        pieces = []
        for index in range(3):
            start = index * block_rows
            stop = start + block_rows
            scores = jnp.dot(tile[start:stop, :head_size], tile[:stop, head_size:2 * head_size].T, preferred_element_type=jnp.float32) * scale
            rows = start + jnp.arange(block_rows, dtype=jnp.int32)[:, None]
            cols = jnp.arange(stop, dtype=jnp.int32)[None, :]
            scores = jnp.where(cols <= rows, scores, -1e30)
            peak = jnp.max(scores, axis=1, keepdims=True)
            expo = jnp.exp(scores - peak)
            weights = (expo / jnp.sum(expo, axis=1, keepdims=True)).astype(jnp.bfloat16)
            pieces.append(jnp.dot(weights, tile[:stop, 2 * head_size:], preferred_element_type=jnp.float32).astype(jnp.bfloat16))
        return jnp.concatenate(pieces, axis=0)

    def one_head(head):
        labels = routes[:, head].astype(jnp.int32)
        order = jnp.argsort(labels * tokens + position).astype(jnp.int32)
        sorted_labels = labels[order]
        counts = jax.ops.segment_sum(jnp.ones((tokens,), jnp.int32), labels, clusters)
        starts = (jnp.cumsum(counts) - counts).astype(jnp.int32)
        slots = position - starts[sorted_labels]
        rows = qkv[:, head, :][order]
        tiles = jnp.zeros((clusters, capacity, width), jnp.bfloat16).at[sorted_labels, slots].set(rows)
        results = lax.map(one_cluster, tiles)
        back = results[sorted_labels, slots]
        return jnp.zeros((tokens, head_size), jnp.bfloat16).at[order].set(back)

    outputs = lax.map(one_head, jnp.arange(heads, dtype=jnp.int32))
    return jnp.transpose(outputs, (1, 0, 2))
```

```python
import functools
import math

import jax
import jax.numpy as jnp
from jax import lax
from jax.experimental import pallas as pl
from jax.experimental.pallas import tpu as pltpu
from jax.sharding import PartitionSpec as P

CLEN = 1024
QB = 256
KB = 512
NEG = -1e30


def attend_kernel(lab_ref, x_ref, o_ref, s_ref, *, head_size, rate):
    block = pl.program_id(0)
    row0 = pl.multiple_of(block * QB, QB)
    tiles = (row0 + QB + KB - 1) // KB
    q = x_ref[pl.ds(row0, QB), :head_size]
    pieces = []
    for part in range(QB // 128):
        lane = lab_ref[pl.ds(block * (QB // 128) + part, 1), :]
        pieces.append(jnp.transpose(jnp.broadcast_to(lane, (128, 128))))
    lab_q = jnp.concatenate(pieces, axis=0)
    rows = row0 + lax.broadcasted_iota(jnp.int32, (QB, 128), 0)
    lanes = lax.broadcasted_iota(jnp.int32, (QB, 128), 1)

    def score(tile, peak):
        col0 = pl.multiple_of(tile * KB, KB)
        k = x_ref[pl.ds(col0, KB), head_size : 2 * head_size]
        s = lax.dot_general(q, k, (((1,), (1,)), ((), ())), preferred_element_type=jnp.float32)
        for part in range(KB // 128):
            lab_k = lab_ref[pl.ds(tile * (KB // 128) + part, 1), :]
            keep = (lab_q == lab_k) & (lanes + (col0 + part * 128) <= rows)
            piece = jnp.where(keep, s[:, part * 128 : (part + 1) * 128], NEG)
            s_ref[:, pl.ds(col0 + part * 128, 128)] = piece
            peak = jnp.maximum(peak, piece)
        return peak

    peak = lax.fori_loop(0, tiles, score, jnp.full((QB, 128), NEG, jnp.float32))
    peak = jnp.broadcast_to(jnp.max(peak, axis=1, keepdims=True), (QB, 128))

    def blend(tile, carry):
        total, acc = carry
        col0 = pl.multiple_of(tile * KB, KB)
        parts = []
        for part in range(KB // 128):
            e = jnp.exp2((s_ref[:, pl.ds(col0 + part * 128, 128)] - peak) * rate)
            total = total + e
            parts.append(e.astype(jnp.bfloat16))
        v = x_ref[pl.ds(col0, KB), 2 * head_size :]
        acc = acc + jnp.dot(jnp.concatenate(parts, axis=1), v, preferred_element_type=jnp.float32)
        return total, acc

    total, acc = lax.fori_loop(
        0,
        tiles,
        blend,
        (jnp.zeros((QB, 128), jnp.float32), jnp.zeros((QB, head_size), jnp.float32)),
    )
    o_ref[...] = (acc / jnp.sum(total, axis=1, keepdims=True)).astype(jnp.bfloat16)


def attend(labels, x, head_size):
    rows, width = x.shape
    rate = math.log2(math.e) / math.sqrt(head_size)
    return pl.pallas_call(
        functools.partial(attend_kernel, head_size=head_size, rate=rate),
        out_shape=jax.ShapeDtypeStruct((rows, head_size), jnp.bfloat16),
        grid=(rows // QB,),
        in_specs=[
            pl.BlockSpec((rows // 128, 128), lambda i: (0, 0)),
            pl.BlockSpec((rows, width), lambda i: (0, 0)),
        ],
        out_specs=pl.BlockSpec((QB, head_size), lambda i: (i, 0)),
        scratch_shapes=[pltpu.VMEM((QB, rows), jnp.float32)],
        compiler_params=pltpu.CompilerParams(
            dimension_semantics=("arbitrary",), vmem_limit_bytes=32 << 20
        ),
        cost_estimate=pl.CostEstimate(
            flops=2 * rows * rows * head_size,
            bytes_accessed=2 * rows * (width + head_size),
            transcendentals=rows * rows // 2,
        ),
        name="attend",
    )(labels, x)


def local(qkv, routes):
    tok, heads, width = qkv.shape
    head_size = width // 3
    nseq = lax.axis_size("seq")
    clusters = nseq * tok // CLEN
    pairs_dev = heads * tok // CLEN
    chunks = max(1, pairs_dev // clusters)
    split = max(1, clusters // pairs_dev)
    share = tok // split

    def exchange(x):
        return lax.all_to_all(x, "seq", split_axis=0, concat_axis=0, tiled=True)

    by_head = jnp.transpose(qkv, (1, 0, 2))
    labels = jnp.transpose(routes)
    if split > 1:
        group = labels // pairs_dev
        member = group[:, :, None] == jnp.arange(split, dtype=jnp.int32)[None, None, :]
        rank = jnp.cumsum(member.astype(jnp.int32), axis=1) - 1
        slot = group * share + jnp.sum(jnp.where(member, rank, 0), axis=2)
        pick = slot[:, None, :] == jnp.arange(tok, dtype=jnp.int32)[None, :, None]
        by_head = jnp.einsum(
            "hst,htd->hsd", pick.astype(jnp.bfloat16), by_head, preferred_element_type=jnp.float32
        ).astype(jnp.bfloat16)
        labels = jnp.sum(jnp.where(pick, labels[:, None, :], 0), axis=2)

    by_head = by_head.reshape(nseq, chunks, share, width)
    labels = exchange(labels.reshape(nseq, chunks, share))
    outs = []
    for chunk in range(chunks):
        rows = exchange(by_head[:, chunk]).reshape(nseq * share, width)
        lab = labels[:, chunk].reshape(nseq * share // 128, 128)
        out = attend(lab, rows, head_size)
        outs.append(exchange(out.reshape(nseq, share, head_size)))
    back = jnp.stack(outs, axis=1).reshape(heads, tok, head_size)
    if split > 1:
        back = jnp.einsum(
            "hst,hsd->htd", pick.astype(jnp.bfloat16), back, preferred_element_type=jnp.float32
        ).astype(jnp.bfloat16)
    return jnp.transpose(back, (1, 0, 2))


def solution(mesh):
    placed = (P(("groups", "seq"), None, None), P(("groups", "seq"), None))
    return jax.shard_map(
        local,
        mesh=mesh,
        in_specs=placed,
        out_specs=P(("groups", "seq"), None, None),
        check_vma=False,
    )
```

```python
import functools
import math

import jax
import jax.numpy as jnp
from jax import lax
from jax.experimental import pallas as pl
from jax.experimental.pallas import tpu as pltpu
from jax.sharding import PartitionSpec as P

CLEN = 1024
QB = 256
NEG = -1e30


def pack_kernel(x_ref, lab_ref, o_ref, *, chunks):
    tok, octet, width = x_ref.shape
    parts = width // 128
    turned = jnp.swapaxes(x_ref[...].astype(jnp.float32), 0, 1).astype(jnp.bfloat16)
    for dst in range(octet // chunks):
        for chunk in range(chunks):
            head = dst * chunks + chunk
            for part in range(parts):
                o_ref[dst, pl.ds((chunk * parts + part) * tok, tok), :] = turned[
                    head, :, part * 128 : (part + 1) * 128
                ]
        labels = lab_ref[dst * chunks : (dst + 1) * chunks, :]
        pad = jnp.zeros((8 - chunks, 128), jnp.float32)
        o_ref[dst, pl.ds(chunks * parts * tok, 8), :] = jnp.concatenate(
            [labels.astype(jnp.float32), pad], axis=0
        ).astype(jnp.bfloat16)


def pack(qkv, labels, chunks):
    tok, heads, width = qkv.shape
    rows = chunks * (width // 128) * tok + 8
    return pl.pallas_call(
        functools.partial(pack_kernel, chunks=chunks),
        out_shape=jax.ShapeDtypeStruct((heads // chunks, rows, 128), jnp.bfloat16),
        grid=(heads // 8,),
        in_specs=[
            pl.BlockSpec((tok, 8, width), lambda i: (0, i, 0)),
            pl.BlockSpec((8, 128), lambda i: (i, 0)),
        ],
        out_specs=pl.BlockSpec((8 // chunks, rows, 128), lambda i: (i, 0, 0)),
        compiler_params=pltpu.CompilerParams(vmem_limit_bytes=32 << 20),
        name="pack",
    )(qkv, labels)


def unpack_kernel(x_ref, o_ref):
    o_ref[...] = jnp.swapaxes(x_ref[...].astype(jnp.float32), 0, 1).astype(jnp.bfloat16)


def unpack(back):
    heads, tok, head_size = back.shape
    return pl.pallas_call(
        unpack_kernel,
        out_shape=jax.ShapeDtypeStruct((tok, heads, head_size), jnp.bfloat16),
        grid=(heads // 8,),
        in_specs=[pl.BlockSpec((8, tok, head_size), lambda i: (i, 0, 0))],
        out_specs=pl.BlockSpec((tok, 8, head_size), lambda i: (0, i, 0)),
        name="unpack",
    )(back)


def attend_kernel(lab_ref, x_ref, o_ref, *, share, rate):
    chunk = pl.program_id(0)
    nseq = x_ref.shape[0]
    rows = nseq * share
    head_size = x_ref.shape[2]
    base = pl.multiple_of(chunk * 3 * share, share)

    def rows_of(part, first, count):
        piece = x_ref[
            first // share : (first + count) // share, pl.ds(base + part * share, share), :
        ]
        return piece.reshape(count, head_size)

    ramp = lax.broadcasted_iota(jnp.int32, (QB, QB), 1) <= lax.broadcasted_iota(
        jnp.int32, (QB, QB), 0
    )
    for block in range(rows // QB):
        row0 = block * QB
        stop = row0 + QB
        q = rows_of(0, row0, QB)
        lab_q = jnp.concatenate(
            [
                jnp.transpose(jnp.broadcast_to(lab_ref[0, i : i + 1, :], (128, 128)))
                for i in range(row0 // 128, stop // 128)
            ],
            axis=0,
        )
        s = lax.dot_general(
            q, rows_of(1, 0, stop), (((1,), (1,)), ((), ())), preferred_element_type=jnp.float32
        )
        pieces = []
        for i in range(stop // 128):
            keep = lab_q == lab_ref[0, i : i + 1, :]
            if i * 128 >= row0:
                keep = keep & ramp[:, i * 128 - row0 : i * 128 - row0 + 128]
            pieces.append(jnp.where(keep, s[:, i * 128 : (i + 1) * 128], NEG))
        peak = functools.reduce(jnp.maximum, pieces)
        peak = jnp.broadcast_to(jnp.max(peak, axis=1, keepdims=True), (QB, 128))
        pieces = [jnp.exp2((piece - peak) * rate) for piece in pieces]
        total = jnp.sum(functools.reduce(jnp.add, pieces), axis=1, keepdims=True)
        weights = jnp.concatenate([piece.astype(jnp.bfloat16) for piece in pieces], axis=1)
        out = jnp.dot(weights, rows_of(2, 0, stop), preferred_element_type=jnp.float32) / total
        o_ref[row0 // share : stop // share] = out.astype(jnp.bfloat16).reshape(
            QB // share, share, head_size
        )


def attend(labels, x, chunks, share):
    nseq, _, head_size = x.shape
    rows = nseq * share
    rate = math.log2(math.e) / math.sqrt(head_size)
    return pl.pallas_call(
        functools.partial(attend_kernel, share=share, rate=rate),
        out_shape=jax.ShapeDtypeStruct((nseq, chunks * share, head_size), jnp.bfloat16),
        grid=(chunks,),
        in_specs=[
            pl.BlockSpec((1, rows // 128, 128), lambda c: (c, 0, 0)),
            pl.BlockSpec(memory_space=pltpu.VMEM),
        ],
        out_specs=pl.BlockSpec((nseq, share, head_size), lambda c: (0, c, 0)),
        compiler_params=pltpu.CompilerParams(
            dimension_semantics=("arbitrary",), vmem_limit_bytes=40 << 20
        ),
        name="attend",
    )(labels, x)


def local(qkv, routes):
    tok, heads, width = qkv.shape
    head_size = width // 3
    nseq = lax.axis_size("seq")
    clusters = nseq * tok // CLEN
    pairs_dev = heads * tok // CLEN
    chunks = max(1, pairs_dev // clusters)
    split = max(1, clusters // pairs_dev)
    share = tok // split

    def exchange(x):
        return lax.all_to_all(x, "seq", split_axis=0, concat_axis=0, tiled=True)

    labels = jnp.transpose(routes)
    if split == 1:
        rows = exchange(pack(qkv, labels, chunks))
    else:
        group = labels // pairs_dev
        member = group[:, :, None] == jnp.arange(split, dtype=jnp.int32)[None, None, :]
        rank = jnp.cumsum(member.astype(jnp.int32), axis=1) - 1
        slot = group * share + jnp.sum(jnp.where(member, rank, 0), axis=2)
        pick = slot[:, None, :] == jnp.arange(tok, dtype=jnp.int32)[None, :, None]
        moved = jnp.einsum(
            "hst,thd->hsd", pick.astype(jnp.bfloat16), qkv, preferred_element_type=jnp.float32
        ).astype(jnp.bfloat16)
        labels = jnp.sum(jnp.where(pick, labels[:, None, :], 0), axis=2)
        moved = moved.reshape(nseq, share, 3, head_size)
        moved = jnp.transpose(moved, (0, 2, 1, 3)).reshape(nseq, 3 * share, head_size)
        extra = labels.reshape(nseq, 1, share).astype(jnp.bfloat16)
        extra = jnp.pad(extra, ((0, 0), (0, 7), (0, head_size - share)))
        rows = exchange(jnp.concatenate([moved, extra], axis=1))
    first = chunks * 3 * share
    arrived = rows[:, first : first + chunks, :share].astype(jnp.int32)
    arrived = jnp.transpose(arrived, (1, 0, 2)).reshape(chunks, nseq * share // 128, 128)
    back = exchange(attend(arrived, rows, chunks, share)).reshape(heads, tok, head_size)
    if split > 1:
        back = jnp.einsum(
            "hst,hsd->htd", pick.astype(jnp.bfloat16), back, preferred_element_type=jnp.float32
        ).astype(jnp.bfloat16)
    return unpack(back)


def solution(mesh):
    placed = (P(("groups", "seq"), None, None), P(("groups", "seq"), None))
    return jax.shard_map(
        local,
        mesh=mesh,
        in_specs=placed,
        out_specs=P(("groups", "seq"), None, None),
        check_vma=False,
    )
```

```python
import functools
import math

import jax
import jax.numpy as jnp
from jax import lax
from jax.experimental import pallas as pl
from jax.experimental.pallas import tpu as pltpu
from jax.sharding import PartitionSpec as P

CLEN = 1024
QB = 256
STEP = 64
NEG = -1e30


def pack_kernel(x_ref, lab_ref, o_ref, *, chunks):
    tok, heads, width = x_ref.shape
    parts = width // 128
    pad = jnp.zeros((8 - chunks, 128), jnp.float32)
    for dst in range(heads // chunks):
        labels = lab_ref[dst * chunks : (dst + 1) * chunks, :]
        o_ref[dst, pl.ds(chunks * parts * tok, 8), :] = jnp.concatenate(
            [labels.astype(jnp.float32), pad], axis=0
        ).astype(jnp.bfloat16)
    for first in range(0, tok, 32):
        piece = x_ref[first : first + 32].astype(jnp.float32)
        turned = jnp.swapaxes(piece, 0, 1).astype(jnp.bfloat16)
        for head in range(heads):
            for part in range(parts):
                row = (head % chunks * parts + part) * tok + first
                o_ref[head // chunks, row : row + 32, :] = turned[
                    head, :, part * 128 : (part + 1) * 128
                ]


def pack(qkv, labels, chunks):
    tok, heads, width = qkv.shape
    rows = chunks * (width // 128) * tok + 8
    whole = pl.BlockSpec(memory_space=pltpu.VMEM)
    return pl.pallas_call(
        functools.partial(pack_kernel, chunks=chunks),
        out_shape=jax.ShapeDtypeStruct((heads // chunks, rows, 128), jnp.bfloat16),
        in_specs=[whole, whole],
        out_specs=whole,
        compiler_params=pltpu.CompilerParams(vmem_limit_bytes=32 << 20),
        name="pack",
    )(qkv, labels)


def unpack_kernel(x_ref, o_ref):
    o_ref[...] = jnp.swapaxes(x_ref[...].astype(jnp.float32), 0, 1).astype(jnp.bfloat16)


def unpack(back):
    heads, tok, head_size = back.shape
    return pl.pallas_call(
        unpack_kernel,
        out_shape=jax.ShapeDtypeStruct((tok, heads, head_size), jnp.bfloat16),
        grid=(tok // STEP,),
        in_specs=[pl.BlockSpec((heads, STEP, head_size), lambda i: (0, i, 0))],
        out_specs=pl.BlockSpec((STEP, heads, head_size), lambda i: (i, 0, 0)),
        name="unpack",
    )(back)


def attend_kernel(lab_ref, x_ref, o_ref, v_ref, *, share, rate):
    nseq, _, head_size = x_ref.shape
    chunks = lab_ref.shape[0]
    rows = nseq * share
    ramp = lax.broadcasted_iota(jnp.int32, (QB, QB), 1) <= lax.broadcasted_iota(
        jnp.int32, (QB, QB), 0
    )

    def rows_of(chunk, part, first, count):
        base = (chunk * 3 + part) * share
        piece = x_ref[first // share : (first + count) // share, base : base + share, :]
        return piece.reshape(count, head_size)

    for chunk in range(chunks):
        v_ref[chunk, :, :head_size] = rows_of(chunk, 2, 0, rows)
        v_ref[chunk, :, head_size:] = jnp.ones((rows, 128), jnp.bfloat16)

    def score(chunk, block):
        return lax.dot_general(
            rows_of(chunk, 0, block * QB, QB),
            rows_of(chunk, 1, 0, (block + 1) * QB),
            (((1,), (1,)), ((), ())),
            preferred_element_type=jnp.float32,
        )

    def weigh(chunk, block, s):
        row0 = block * QB
        stop = row0 + QB
        lab_q = jnp.concatenate(
            [
                jnp.transpose(jnp.broadcast_to(lab_ref[chunk, i : i + 1, :], (128, 128)))
                for i in range(row0 // 128, stop // 128)
            ],
            axis=0,
        )
        pieces = []
        for i in range(stop // 128):
            keep = lab_q == lab_ref[chunk, i : i + 1, :]
            if i * 128 >= row0:
                keep = keep & ramp[:, i * 128 - row0 : i * 128 - row0 + 128]
            pieces.append(jnp.where(keep, s[:, i * 128 : (i + 1) * 128], NEG))
        peak = functools.reduce(jnp.maximum, pieces)
        peak = jnp.broadcast_to(jnp.max(peak, axis=1, keepdims=True), (QB, 128))
        pieces = [jnp.exp2((piece - peak) * rate).astype(jnp.bfloat16) for piece in pieces]
        return jnp.concatenate(pieces, axis=1)

    def blend(chunk, block, weights):
        row0 = block * QB
        stop = row0 + QB
        both = jnp.dot(weights, v_ref[chunk, :stop, :], preferred_element_type=jnp.float32)
        out = both[:, :head_size] / both[:, head_size:]
        o_ref[row0 // share : stop // share, chunk * share : (chunk + 1) * share] = out.astype(
            jnp.bfloat16
        ).reshape(QB // share, share, head_size)

    blocks = rows // QB
    tasks = [
        (chunk, step if chunk % 2 == 0 else blocks - 1 - step)
        for step in range(blocks)
        for chunk in range(chunks)
    ]
    ahead = score(*tasks[0])
    behind = None
    for place, task in enumerate(tasks):
        s = ahead
        if place + 1 < len(tasks):
            ahead = score(*tasks[place + 1])
        weights = weigh(*task, s)
        if behind is not None:
            blend(*behind)
        behind = (*task, weights)
    blend(*behind)


def attend(labels, x, chunks, share):
    nseq, _, head_size = x.shape
    rows = nseq * share
    rate = math.log2(math.e) / math.sqrt(head_size)
    whole = pl.BlockSpec(memory_space=pltpu.VMEM)
    return pl.pallas_call(
        functools.partial(attend_kernel, share=share, rate=rate),
        out_shape=jax.ShapeDtypeStruct((nseq, chunks * share, head_size), jnp.bfloat16),
        in_specs=[whole, whole],
        out_specs=whole,
        scratch_shapes=[pltpu.VMEM((chunks, rows, head_size + 128), jnp.bfloat16)],
        compiler_params=pltpu.CompilerParams(vmem_limit_bytes=40 << 20),
        name="attend",
    )(labels, x)


def local(qkv, routes):
    tok, heads, width = qkv.shape
    head_size = width // 3
    nseq = lax.axis_size("seq")
    clusters = nseq * tok // CLEN
    pairs_dev = heads * tok // CLEN
    chunks = max(1, pairs_dev // clusters)
    split = max(1, clusters // pairs_dev)
    share = tok // split

    def exchange(x):
        return lax.all_to_all(x, "seq", split_axis=0, concat_axis=0, tiled=True)

    labels = jnp.transpose(routes)
    if split == 1:
        rows = exchange(pack(qkv, labels, chunks))
    else:
        group = labels // pairs_dev
        member = group[:, :, None] == jnp.arange(split, dtype=jnp.int32)[None, None, :]
        rank = jnp.cumsum(member.astype(jnp.int32), axis=1) - 1
        slot = group * share + jnp.sum(jnp.where(member, rank, 0), axis=2)
        pick = slot[:, None, :] == jnp.arange(tok, dtype=jnp.int32)[None, :, None]
        moved = jnp.einsum(
            "hst,thd->hsd", pick.astype(jnp.bfloat16), qkv, preferred_element_type=jnp.float32
        ).astype(jnp.bfloat16)
        labels = jnp.sum(jnp.where(pick, labels[:, None, :], 0), axis=2)
        moved = moved.reshape(nseq, share, 3, head_size)
        moved = jnp.transpose(moved, (0, 2, 1, 3)).reshape(nseq, 3 * share, head_size)
        extra = labels.reshape(nseq, 1, share).astype(jnp.bfloat16)
        extra = jnp.pad(extra, ((0, 0), (0, 7), (0, head_size - share)))
        rows = exchange(jnp.concatenate([moved, extra], axis=1))
    first = chunks * 3 * share
    arrived = rows[:, first : first + chunks, :share].astype(jnp.int32)
    arrived = jnp.transpose(arrived, (1, 0, 2)).reshape(chunks, nseq * share // 128, 128)
    back = exchange(attend(arrived, rows, chunks, share)).reshape(heads, tok, head_size)
    if split > 1:
        back = jnp.einsum(
            "hst,hsd->htd", pick.astype(jnp.bfloat16), back, preferred_element_type=jnp.float32
        ).astype(jnp.bfloat16)
    return unpack(back)


def solution(mesh):
    placed = (P(("groups", "seq"), None, None), P(("groups", "seq"), None))
    return jax.shard_map(
        local,
        mesh=mesh,
        in_specs=placed,
        out_specs=P(("groups", "seq"), None, None),
        check_vma=False,
    )
```

```python
import functools
import math

import jax
import jax.numpy as jnp
from jax import lax
from jax.experimental import pallas as pl
from jax.experimental.pallas import tpu as pltpu
from jax.sharding import PartitionSpec as P

CLEN = 1024
QB = 256
STEP = 64
NEG = -1e30


def pack_kernel(x_ref, lab_ref, o_ref, *, chunks):
    tok, heads, width = x_ref.shape
    parts = width // 128
    pad = jnp.zeros((8 - chunks, 128), jnp.float32)
    for dst in range(heads // chunks):
        labels = lab_ref[dst * chunks : (dst + 1) * chunks, :]
        o_ref[dst, pl.ds(chunks * parts * tok, 8), :] = jnp.concatenate(
            [labels.astype(jnp.float32), pad], axis=0
        ).astype(jnp.bfloat16)
    for first in range(0, tok, 32):
        piece = x_ref[first : first + 32].astype(jnp.float32)
        turned = jnp.swapaxes(piece, 0, 1).astype(jnp.bfloat16)
        for head in range(heads):
            for part in range(parts):
                row = (head % chunks * parts + part) * tok + first
                o_ref[head // chunks, row : row + 32, :] = turned[
                    head, :, part * 128 : (part + 1) * 128
                ]


def pack(qkv, labels, chunks):
    tok, heads, width = qkv.shape
    rows = chunks * (width // 128) * tok + 8
    whole = pl.BlockSpec(memory_space=pltpu.VMEM)
    return pl.pallas_call(
        functools.partial(pack_kernel, chunks=chunks),
        out_shape=jax.ShapeDtypeStruct((heads // chunks, rows, 128), jnp.bfloat16),
        in_specs=[whole, whole],
        out_specs=whole,
        compiler_params=pltpu.CompilerParams(vmem_limit_bytes=32 << 20),
        name="pack",
    )(qkv, labels)


def unpack_kernel(x_ref, o_ref):
    o_ref[...] = jnp.swapaxes(x_ref[...].astype(jnp.float32), 0, 1).astype(jnp.bfloat16)


def unpack(back):
    heads, tok, head_size = back.shape
    return pl.pallas_call(
        unpack_kernel,
        out_shape=jax.ShapeDtypeStruct((tok, heads, head_size), jnp.bfloat16),
        grid=(tok // STEP,),
        in_specs=[pl.BlockSpec((heads, STEP, head_size), lambda i: (0, i, 0))],
        out_specs=pl.BlockSpec((STEP, heads, head_size), lambda i: (i, 0, 0)),
        name="unpack",
    )(back)


def attend_kernel(lab_ref, x_ref, o_ref, v_ref, *, share, rate):
    nseq, _, head_size = x_ref.shape
    chunks = lab_ref.shape[0]
    rows = nseq * share
    ramp = lax.broadcasted_iota(jnp.int32, (QB, QB), 1) <= lax.broadcasted_iota(
        jnp.int32, (QB, QB), 0
    )

    def rows_of(chunk, part, first, count):
        base = (chunk * 3 + part) * share
        piece = x_ref[first // share : (first + count) // share, base : base + share, :]
        return piece.reshape(count, head_size)

    for chunk in range(chunks):
        v_ref[chunk, :, :head_size] = rows_of(chunk, 2, 0, rows)
        v_ref[chunk, :, head_size:] = jnp.ones((rows, 128), jnp.bfloat16)

    def score(chunk, block):
        return lax.dot_general(
            rows_of(chunk, 0, block * QB, QB),
            rows_of(chunk, 1, 0, (block + 1) * QB),
            (((1,), (1,)), ((), ())),
            preferred_element_type=jnp.float32,
        )

    def weigh(chunk, block, s):
        row0 = block * QB
        stop = row0 + QB
        lab_q = jnp.concatenate(
            [
                jnp.transpose(jnp.broadcast_to(lab_ref[chunk, i : i + 1, :], (128, 128)))
                for i in range(row0 // 128, stop // 128)
            ],
            axis=0,
        )
        pieces = []
        for i in range(stop // 128):
            keep = lab_q == lab_ref[chunk, i : i + 1, :]
            if i * 128 >= row0:
                keep = keep & ramp[:, i * 128 - row0 : i * 128 - row0 + 128]
            pieces.append(jnp.where(keep, s[:, i * 128 : (i + 1) * 128], NEG))
        peak = functools.reduce(jnp.maximum, pieces)
        peak = jnp.broadcast_to(jnp.max(peak, axis=1, keepdims=True), (QB, 128))
        pieces = [jnp.exp2((piece - peak) * rate).astype(jnp.bfloat16) for piece in pieces]
        return jnp.concatenate(pieces, axis=1)

    def blend(chunk, block, weights):
        row0 = block * QB
        stop = row0 + QB
        both = jnp.dot(weights, v_ref[chunk, :stop, :], preferred_element_type=jnp.float32)
        out = both[:, :head_size] / both[:, head_size:]
        o_ref[row0 // share : stop // share, chunk * share : (chunk + 1) * share] = out.astype(
            jnp.bfloat16
        ).reshape(QB // share, share, head_size)

    blocks = rows // QB
    tasks = [
        (chunk, step if chunk % 2 == 0 else blocks - 1 - step)
        for step in range(blocks)
        for chunk in range(chunks)
    ]
    ahead = score(*tasks[0])
    behind = None
    for place, task in enumerate(tasks):
        s = ahead
        if place + 1 < len(tasks):
            ahead = score(*tasks[place + 1])
        weights = weigh(*task, s)
        if behind is not None:
            blend(*behind)
        behind = (*task, weights)
    blend(*behind)


def attend(labels, x, chunks, share):
    nseq, _, head_size = x.shape
    rows = nseq * share
    rate = math.log2(math.e) / math.sqrt(head_size)
    whole = pl.BlockSpec(memory_space=pltpu.VMEM)
    return pl.pallas_call(
        functools.partial(attend_kernel, share=share, rate=rate),
        out_shape=jax.ShapeDtypeStruct((nseq, chunks * share, head_size), jnp.bfloat16),
        in_specs=[whole, whole],
        out_specs=whole,
        scratch_shapes=[pltpu.VMEM((chunks, rows, head_size + 128), jnp.bfloat16)],
        compiler_params=pltpu.CompilerParams(vmem_limit_bytes=40 << 20),
        name="attend",
    )(labels, x)


def spread_kernel(me_ref, x_ref, lab_ref, cross_ref, *rest):
    near_refs, turn_ref = rest[:-1], rest[-1]
    tok, heads, width = x_ref.shape
    nseq = cross_ref.shape[0]
    half = nseq // 2
    me = me_ref[0]
    pad = jnp.zeros((4, 128), jnp.float32)
    for dst in range(nseq):
        other = dst ^ half
        labels = [lab_ref[2 * dst : 2 * dst + 2, :], lab_ref[2 * other : 2 * other + 2, :]]
        labels = [piece.astype(jnp.float32) for piece in labels]
        cross_ref[dst, 4 * tok : 4 * tok + 8, :] = jnp.concatenate(labels + [pad], axis=0).astype(
            jnp.bfloat16
        )
    for first in range(0, tok, 32):
        piece = x_ref[first : first + 32].astype(jnp.float32)
        turned = jnp.swapaxes(piece, 0, 1).astype(jnp.bfloat16)
        for head in range(heads):
            for part in range(3):
                value = turned[head, :, part * 128 : (part + 1) * 128]
                turn_ref[head, part, first : first + 32, :] = value
                side = 0 if head // 2 < half else 2
                if part == 1 or part == side:
                    row = (head % 2 + (0 if part == 1 else 2)) * tok + first
                    cross_ref[head // 2, row : row + 32, :] = value
    near_part = jnp.where(me >= half, 0, 2)
    for k, near_ref in enumerate(near_refs):
        dst = me ^ k
        other = dst ^ half
        for j in range(2):
            near_ref[j * tok : (j + 1) * tok, :] = turn_ref[2 * dst + j, near_part]
            for part in range(3):
                row = (2 + 2 * part + j) * tok
                near_ref[row : row + tok, :] = turn_ref[2 * other + j, part]


def spread(me, qkv, labels, nseq):
    tok, heads, width = qkv.shape
    whole = pl.BlockSpec(memory_space=pltpu.VMEM)
    near = jax.ShapeDtypeStruct((8 * tok, 128), jnp.bfloat16)
    out = pl.pallas_call(
        spread_kernel,
        out_shape=[jax.ShapeDtypeStruct((nseq, 4 * tok + 8, 128), jnp.bfloat16)]
        + [near] * (nseq // 2),
        in_specs=[pl.BlockSpec(memory_space=pltpu.SMEM), whole, whole],
        out_specs=[whole] * (1 + nseq // 2),
        scratch_shapes=[pltpu.VMEM((heads, 3, tok, 128), jnp.bfloat16)],
        compiler_params=pltpu.CompilerParams(vmem_limit_bytes=32 << 20),
        name="spread",
    )(me, qkv, labels)
    return out[0], out[1:]


def run_tasks(tasks, score, weigh, blend):
    ahead = score(*tasks[0])
    behind = None
    for place, task in enumerate(tasks):
        s = ahead
        if place + 1 < len(tasks):
            ahead = score(*tasks[place + 1])
        found = weigh(*task, s)
        if behind is not None:
            blend(*behind)
        behind = (*task, *found)
    blend(*behind)


def dot_t(a, b):
    return lax.dot_general(a, b, (((1,), (1,)), ((), ())), preferred_element_type=jnp.float32)


def soften(s, lab_q, lab_k, diagonal, rate):
    pieces = []
    for i, lab in enumerate(lab_k):
        keep = lab_q == lab
        if diagonal is not None and i * 128 >= diagonal:
            lanes = lax.broadcasted_iota(jnp.int32, (QB, 128), 1) + (i * 128 - diagonal)
            keep = keep & (lanes <= lax.broadcasted_iota(jnp.int32, (QB, 128), 0))
        pieces.append(jnp.where(keep, s[:, i * 128 : (i + 1) * 128], NEG))
    peak = functools.reduce(jnp.maximum, pieces)
    peak = jnp.broadcast_to(jnp.max(peak, axis=1, keepdims=True), (QB, 128))
    pieces = [jnp.exp2((piece - peak) * rate).astype(jnp.bfloat16) for piece in pieces]
    return jnp.concatenate(pieces, axis=1), peak


def columns(rows):
    return jnp.concatenate(
        [jnp.transpose(jnp.broadcast_to(row, (128, 128))) for row in rows], axis=0
    )


def three_parts(stats):
    rows = []
    for row in stats:
        for _ in range(3):
            part = row.astype(jnp.bfloat16).astype(jnp.float32)
            rows.append(part)
            row = row - part
    rows.append(jnp.zeros((8 - len(rows), 128), jnp.float32))
    return jnp.concatenate(rows, axis=0).astype(jnp.bfloat16)


def own_kernel(me_ref, lab_ref, x_ref, *rest, tok, rate):
    nseq = x_ref.shape[0]
    half = nseq // 2
    span = half * tok
    near_refs, o_ref = rest[:half], rest[half]
    q_ref, v_ref, num_ref, sum_ref, peak_ref, stat_ref = rest[half + 1 :]
    me = me_ref[0]
    upper = me >= half
    up = upper.astype(jnp.int32)
    for j in range(2):
        for slot in range(2):
            v_ref[j, slot, :, 128:] = jnp.ones((span, 128), jnp.bfloat16)

    @pl.when(upper)
    def _():
        for j in range(2):
            for k, near_ref in enumerate(near_refs):
                place = pl.multiple_of(((me ^ k) % half) * tok, tok)
                q_ref[j, 1, pl.ds(place, tok), :] = near_ref[j * tok : (j + 1) * tok, :]
            for slot in range(2):
                v_ref[j, slot, :, :128] = x_ref[
                    slot * half : (slot + 1) * half, (2 + j) * tok : (3 + j) * tok, :
                ].reshape(span, 128)

    @pl.when(jnp.logical_not(upper))
    def _():
        for j in range(2):
            for k, near_ref in enumerate(near_refs):
                place = pl.multiple_of(((me ^ k) % half) * tok, tok)
                v_ref[j, 0, pl.ds(place, tok), :128] = near_ref[j * tok : (j + 1) * tok, :]
            for slot in range(2):
                q_ref[j, slot] = x_ref[
                    slot * half : (slot + 1) * half, (2 + j) * tok : (3 + j) * tok, :
                ].reshape(span, 128)

    def keys(j, first, count):
        return x_ref[pl.ds(first, count), j * tok : (j + 1) * tok, :].reshape(count * tok, 128)

    def lab_of(j, first, count):
        return [lab_ref[j, pl.ds(first + i, 1), :] for i in range(count)]

    per = QB // tok

    def score(cross, j, block):
        rows = pl.ds(block * QB, QB)
        if cross:
            return dot_t(q_ref[j, 1, rows, :], keys(j, 0, half))
        return dot_t(q_ref[j, up, rows, :], keys(j, up * half, (block + 1) * per))

    def weigh(cross, j, block, s):
        if cross:
            lab_q = columns(lab_of(j, half + block * per, per))
            return soften(s, lab_q, lab_of(j, 0, half), None, rate)
        lab_q = columns(lab_of(j, up * half + block * per, per))
        lab_k = lab_of(j, up * half, (block + 1) * per)
        return soften(s, lab_q, lab_k, block * QB, rate)

    def blend(cross, j, block, weights, peak):
        rows = pl.ds(block * QB, QB)
        if cross:
            both = jnp.dot(weights, v_ref[j, 0], preferred_element_type=jnp.float32)
            num, total = both[:, :128], both[:, 128:]
            num_ref[j, rows, :] = num
            sum_ref[j, rows, :] = total
            peak_ref[j, rows, :] = peak
            lse = peak * rate + jnp.log2(total)
            for i in range(per):
                turned = jnp.transpose(lse[i * tok : (i + 1) * tok, :])
                stat_ref[j, block * per + i : block * per + i + 1, :] = turned[:1, :]
            out = num / total
            first = (1 - up) * half + block * per
        else:
            both = jnp.dot(
                weights, v_ref[j, up, : (block + 1) * QB, :], preferred_element_type=jnp.float32
            )
            far = jnp.where(upper, peak_ref[j, rows, :], NEG)
            top = jnp.maximum(peak, far)
            here = jnp.exp2((peak - top) * rate)
            there = jnp.exp2((far - top) * rate)
            num = both[:, :128] * here + num_ref[j, rows, :] * there
            out = num / (both[:, 128:] * here + sum_ref[j, rows, :] * there)
            first = up * half + block * per
        o_ref[pl.ds(first, per), j * tok : (j + 1) * tok, :] = out.astype(jnp.bfloat16).reshape(
            per, tok, 128
        )

    blocks = span // QB
    tasks = [(True, j, block) for block in range(blocks) for j in range(2)]
    tasks += [
        (False, j, block if j == 0 else blocks - 1 - block)
        for block in range(blocks)
        for j in range(2)
    ]
    run_tasks(tasks, score, weigh, blend)
    for i in range(half):
        stats = three_parts([stat_ref[j, i : i + 1, :] for j in range(2)])
        o_ref[(1 - up) * half + i, 2 * tok : 2 * tok + 8, :] = stats
        o_ref[up * half + i, 2 * tok : 2 * tok + 8, :] = jnp.zeros((8, 128), jnp.bfloat16)


def own(me, labels, x, near, tok, rate):
    nseq = x.shape[0]
    half = nseq // 2
    span = half * tok
    whole = pl.BlockSpec(memory_space=pltpu.VMEM)
    return pl.pallas_call(
        functools.partial(own_kernel, tok=tok, rate=rate),
        out_shape=jax.ShapeDtypeStruct((nseq, 2 * tok + 8, 128), jnp.bfloat16),
        in_specs=[pl.BlockSpec(memory_space=pltpu.SMEM)] + [whole] * (2 + half),
        out_specs=whole,
        scratch_shapes=[
            pltpu.VMEM((2, 2, span, 128), jnp.bfloat16),
            pltpu.VMEM((2, 2, span, 256), jnp.bfloat16),
            pltpu.VMEM((2, span, 128), jnp.float32),
            pltpu.VMEM((2, span, 128), jnp.float32),
            pltpu.VMEM((2, span, 128), jnp.float32),
            pltpu.VMEM((2, half, 128), jnp.float32),
        ],
        compiler_params=pltpu.CompilerParams(vmem_limit_bytes=40 << 20),
        name="own",
    )(me, labels, x, *near)


def partner_kernel(me_ref, lab_ref, *rest, tok, rate):
    half = (len(rest) - 5) // 2
    near_refs, o_refs = rest[:half], rest[half : 2 * half]
    q_ref, k_ref, v_ref, out_ref, stat_ref = rest[2 * half :]
    span = half * tok
    me = me_ref[0]
    up = (me >= half).astype(jnp.int32)
    for j in range(2):
        v_ref[j, :, 128:] = jnp.ones((span, 128), jnp.bfloat16)
        for k, near_ref in enumerate(near_refs):
            place = pl.ds(pl.multiple_of(((me ^ k) % half) * tok, tok), tok)
            q_ref[j, place, :] = near_ref[(2 + j) * tok : (3 + j) * tok, :]
            k_ref[j, place, :] = near_ref[(4 + j) * tok : (5 + j) * tok, :]
            v_ref[j, place, :128] = near_ref[(6 + j) * tok : (7 + j) * tok, :]

    def lab_of(j, first, count):
        return [lab_ref[2 + j, pl.ds(up * half + first + i, 1), :] for i in range(count)]

    per = QB // tok

    def score(j, block):
        return dot_t(q_ref[j, pl.ds(block * QB, QB), :], k_ref[j, : (block + 1) * QB, :])

    def weigh(j, block, s):
        lab_q = columns(lab_of(j, block * per, per))
        return soften(s, lab_q, lab_of(j, 0, (block + 1) * per), block * QB, rate)

    def blend(j, block, weights, peak):
        both = jnp.dot(
            weights, v_ref[j, : (block + 1) * QB, :], preferred_element_type=jnp.float32
        )
        num, total = both[:, :128], both[:, 128:]
        lse = peak * rate + jnp.log2(total)
        out = (num / total).astype(jnp.bfloat16)
        for i in range(per):
            turned = jnp.transpose(lse[i * tok : (i + 1) * tok, :])
            stat_ref[j, block * per + i : block * per + i + 1, :] = turned[:1, :]
            out_ref[block * per + i, j * tok : (j + 1) * tok, :] = out[i * tok : (i + 1) * tok, :]

    blocks = span // QB
    tasks = [
        (j, block if j == 0 else blocks - 1 - block) for block in range(blocks) for j in range(2)
    ]
    run_tasks(tasks, score, weigh, blend)
    for i in range(half):
        stats = three_parts([stat_ref[j, i : i + 1, :] for j in range(2)])
        out_ref[i, 2 * tok : 2 * tok + 8, :] = stats
    for k, o_ref in enumerate(o_refs):
        o_ref[...] = out_ref[(me ^ k) % half]


def partner(me, labels, near, tok, rate):
    half = len(near)
    span = half * tok
    whole = pl.BlockSpec(memory_space=pltpu.VMEM)
    return pl.pallas_call(
        functools.partial(partner_kernel, tok=tok, rate=rate),
        out_shape=[jax.ShapeDtypeStruct((2 * tok + 8, 128), jnp.bfloat16)] * half,
        in_specs=[pl.BlockSpec(memory_space=pltpu.SMEM)] + [whole] * (1 + half),
        out_specs=[whole] * half,
        scratch_shapes=[
            pltpu.VMEM((2, span, 128), jnp.bfloat16),
            pltpu.VMEM((2, span, 128), jnp.bfloat16),
            pltpu.VMEM((2, span, 256), jnp.bfloat16),
            pltpu.VMEM((half, 2 * tok + 8, 128), jnp.bfloat16),
            pltpu.VMEM((2, half, 128), jnp.float32),
        ],
        compiler_params=pltpu.CompilerParams(vmem_limit_bytes=32 << 20),
        name="partner",
    )(me, labels, *near)


def merge_kernel(me_ref, x_ref, *rest, tok):
    nseq = x_ref.shape[0]
    half = nseq // 2
    near_refs, o_ref, head_ref = rest[:half], rest[half], rest[half + 1]
    me = me_ref[0]
    upper = me >= half
    up = upper.astype(jnp.int32)
    down = 1 - up
    heads = 2 * nseq
    for i in range(half):
        for j in range(2):
            head_ref[up * (heads // 2) + 2 * i + j] = x_ref[
                up * half + i, j * tok : (j + 1) * tok, :
            ].astype(jnp.float32)
    for k, near_ref in enumerate(near_refs):
        place = (me ^ k) % half
        far_stats = x_ref[down * half + place, 2 * tok : 2 * tok + 8, :].astype(jnp.float32)
        near_stats = near_ref[2 * tok : 2 * tok + 8, :].astype(jnp.float32)
        for j in range(2):
            near_lse = sum(near_stats[3 * j + c : 3 * j + c + 1, :] for c in range(3))
            far_lse = sum(far_stats[3 * j + c : 3 * j + c + 1, :] for c in range(3))
            weight = jnp.where(upper, 1.0 / (1.0 + jnp.exp2(near_lse - far_lse)), 0.0)
            weight = jnp.transpose(jnp.broadcast_to(weight, (128, tok)))
            far = x_ref[down * half + place, j * tok : (j + 1) * tok, :].astype(jnp.float32)
            near = near_ref[j * tok : (j + 1) * tok, :].astype(jnp.float32)
            head_ref[down * (heads // 2) + 2 * place + j] = near + (far - near) * weight
    for first in range(0, tok, 32):
        piece = head_ref[:, first : first + 32, :]
        o_ref[first : first + 32] = jnp.swapaxes(piece, 0, 1).astype(jnp.bfloat16)


def merge(me, x, near, tok):
    nseq = x.shape[0]
    whole = pl.BlockSpec(memory_space=pltpu.VMEM)
    return pl.pallas_call(
        functools.partial(merge_kernel, tok=tok),
        out_shape=jax.ShapeDtypeStruct((tok, 2 * nseq, 128), jnp.bfloat16),
        in_specs=[pl.BlockSpec(memory_space=pltpu.SMEM)] + [whole] * (1 + nseq // 2),
        out_specs=whole,
        scratch_shapes=[pltpu.VMEM((2 * nseq, tok, 128), jnp.float32)],
        compiler_params=pltpu.CompilerParams(vmem_limit_bytes=32 << 20),
        name="merge",
    )(me, x, *near)


def two_halves(qkv, labels):
    tok, heads, width = qkv.shape
    nseq = lax.axis_size("seq")
    rate = math.log2(math.e) / math.sqrt(width // 3)
    me = lax.axis_index("seq").astype(jnp.int32).reshape(1)

    def exchange(x):
        return lax.all_to_all(x, "seq", split_axis=0, concat_axis=0, tiled=True)

    def swap(blocks):
        moved = [
            lax.ppermute(block, "seq", [(i, i ^ k) for i in range(nseq)])
            for k, block in enumerate(blocks)
            if k
        ]
        return [blocks[0]] + moved

    cross, near = spread(me, qkv, labels, nseq)
    near = swap(near)
    cross = exchange(cross)
    labels = jnp.transpose(cross[:, 4 * tok : 4 * tok + 4, :].astype(jnp.int32), (1, 0, 2))
    back = exchange(own(me, labels, cross, near, tok, rate))
    near_back = swap(partner(me, labels, near, tok, rate))
    return merge(me, back, near_back, tok)


def local(qkv, routes):
    tok, heads, width = qkv.shape
    head_size = width // 3
    nseq = lax.axis_size("seq")
    clusters = nseq * tok // CLEN
    pairs_dev = heads * tok // CLEN
    chunks = max(1, pairs_dev // clusters)
    split = max(1, clusters // pairs_dev)
    share = tok // split

    def exchange(x):
        return lax.all_to_all(x, "seq", split_axis=0, concat_axis=0, tiled=True)

    labels = jnp.transpose(routes)
    paired = nseq & (nseq - 1) == 0 and nseq * tok // 2 % QB == 0
    if split == 1 and chunks == 2 and paired and tok == 128 and head_size == 128:
        return two_halves(qkv, labels)
    if split == 1:
        rows = exchange(pack(qkv, labels, chunks))
    else:
        group = labels // pairs_dev
        member = group[:, :, None] == jnp.arange(split, dtype=jnp.int32)[None, None, :]
        rank = jnp.cumsum(member.astype(jnp.int32), axis=1) - 1
        slot = group * share + jnp.sum(jnp.where(member, rank, 0), axis=2)
        pick = slot[:, None, :] == jnp.arange(tok, dtype=jnp.int32)[None, :, None]
        moved = jnp.einsum(
            "hst,thd->hsd", pick.astype(jnp.bfloat16), qkv, preferred_element_type=jnp.float32
        ).astype(jnp.bfloat16)
        labels = jnp.sum(jnp.where(pick, labels[:, None, :], 0), axis=2)
        moved = moved.reshape(nseq, share, 3, head_size)
        moved = jnp.transpose(moved, (0, 2, 1, 3)).reshape(nseq, 3 * share, head_size)
        extra = labels.reshape(nseq, 1, share).astype(jnp.bfloat16)
        extra = jnp.pad(extra, ((0, 0), (0, 7), (0, head_size - share)))
        rows = exchange(jnp.concatenate([moved, extra], axis=1))
    first = chunks * 3 * share
    arrived = rows[:, first : first + chunks, :share].astype(jnp.int32)
    arrived = jnp.transpose(arrived, (1, 0, 2)).reshape(chunks, nseq * share // 128, 128)
    back = exchange(attend(arrived, rows, chunks, share)).reshape(heads, tok, head_size)
    if split > 1:
        back = jnp.einsum(
            "hst,hsd->htd", pick.astype(jnp.bfloat16), back, preferred_element_type=jnp.float32
        ).astype(jnp.bfloat16)
    return unpack(back)


def solution(mesh):
    placed = (P(("groups", "seq"), None, None), P(("groups", "seq"), None))
    return jax.shard_map(
        local,
        mesh=mesh,
        in_specs=placed,
        out_specs=P(("groups", "seq"), None, None),
        check_vma=False,
    )
```

```python
import functools
import math

import jax
import jax.numpy as jnp
from jax import lax
from jax.experimental import pallas as pl
from jax.experimental.pallas import tpu as pltpu
from jax.sharding import PartitionSpec as P

CLEN = 1024
QB = 256
STEP = 64
SPREAD_MB = 12
NEG = -1e30


def pack_kernel(x_ref, lab_ref, o_ref, *, chunks):
    tok, heads, width = x_ref.shape
    parts = width // 128
    pad = jnp.zeros((8 - chunks, 128), jnp.float32)
    for dst in range(heads // chunks):
        labels = lab_ref[dst * chunks : (dst + 1) * chunks, :]
        o_ref[dst, pl.ds(chunks * parts * tok, 8), :] = jnp.concatenate(
            [labels.astype(jnp.float32), pad], axis=0
        ).astype(jnp.bfloat16)
    for first in range(0, tok, 32):
        piece = x_ref[first : first + 32].astype(jnp.float32)
        turned = jnp.swapaxes(piece, 0, 1).astype(jnp.bfloat16)
        for head in range(heads):
            for part in range(parts):
                row = (head % chunks * parts + part) * tok + first
                o_ref[head // chunks, row : row + 32, :] = turned[
                    head, :, part * 128 : (part + 1) * 128
                ]


def pack(qkv, labels, chunks):
    tok, heads, width = qkv.shape
    rows = chunks * (width // 128) * tok + 8
    whole = pl.BlockSpec(memory_space=pltpu.VMEM)
    return pl.pallas_call(
        functools.partial(pack_kernel, chunks=chunks),
        out_shape=jax.ShapeDtypeStruct((heads // chunks, rows, 128), jnp.bfloat16),
        in_specs=[whole, whole],
        out_specs=whole,
        compiler_params=pltpu.CompilerParams(vmem_limit_bytes=32 << 20),
        name="pack",
    )(qkv, labels)


def unpack_kernel(x_ref, o_ref):
    o_ref[...] = jnp.swapaxes(x_ref[...].astype(jnp.float32), 0, 1).astype(jnp.bfloat16)


def unpack(back):
    heads, tok, head_size = back.shape
    return pl.pallas_call(
        unpack_kernel,
        out_shape=jax.ShapeDtypeStruct((tok, heads, head_size), jnp.bfloat16),
        grid=(tok // STEP,),
        in_specs=[pl.BlockSpec((heads, STEP, head_size), lambda i: (0, i, 0))],
        out_specs=pl.BlockSpec((STEP, heads, head_size), lambda i: (i, 0, 0)),
        name="unpack",
    )(back)


def attend_kernel(lab_ref, x_ref, o_ref, v_ref, *, share, rate):
    nseq, _, head_size = x_ref.shape
    chunks = lab_ref.shape[0]
    rows = nseq * share
    ramp = lax.broadcasted_iota(jnp.int32, (QB, QB), 1) <= lax.broadcasted_iota(
        jnp.int32, (QB, QB), 0
    )

    def rows_of(chunk, part, first, count):
        base = (chunk * 3 + part) * share
        piece = x_ref[first // share : (first + count) // share, base : base + share, :]
        return piece.reshape(count, head_size)

    for chunk in range(chunks):
        v_ref[chunk, :, :head_size] = rows_of(chunk, 2, 0, rows)
        v_ref[chunk, :, head_size:] = jnp.ones((rows, 128), jnp.bfloat16)

    def score(chunk, block):
        return lax.dot_general(
            rows_of(chunk, 0, block * QB, QB),
            rows_of(chunk, 1, 0, (block + 1) * QB),
            (((1,), (1,)), ((), ())),
            preferred_element_type=jnp.float32,
        )

    def weigh(chunk, block, s):
        row0 = block * QB
        stop = row0 + QB
        lab_q = jnp.concatenate(
            [
                jnp.transpose(jnp.broadcast_to(lab_ref[chunk, i : i + 1, :], (128, 128)))
                for i in range(row0 // 128, stop // 128)
            ],
            axis=0,
        )
        pieces = []
        for i in range(stop // 128):
            keep = lab_q == lab_ref[chunk, i : i + 1, :]
            if i * 128 >= row0:
                keep = keep & ramp[:, i * 128 - row0 : i * 128 - row0 + 128]
            pieces.append(jnp.where(keep, s[:, i * 128 : (i + 1) * 128], NEG))
        peak = functools.reduce(jnp.maximum, pieces)
        peak = jnp.broadcast_to(jnp.max(peak, axis=1, keepdims=True), (QB, 128))
        pieces = [jnp.exp2((piece - peak) * rate).astype(jnp.bfloat16) for piece in pieces]
        return jnp.concatenate(pieces, axis=1)

    def blend(chunk, block, weights):
        row0 = block * QB
        stop = row0 + QB
        both = jnp.dot(weights, v_ref[chunk, :stop, :], preferred_element_type=jnp.float32)
        out = both[:, :head_size] / both[:, head_size:]
        o_ref[row0 // share : stop // share, chunk * share : (chunk + 1) * share] = out.astype(
            jnp.bfloat16
        ).reshape(QB // share, share, head_size)

    blocks = rows // QB
    tasks = [
        (chunk, step if chunk % 2 == 0 else blocks - 1 - step)
        for step in range(blocks)
        for chunk in range(chunks)
    ]
    ahead = score(*tasks[0])
    behind = None
    for place, task in enumerate(tasks):
        s = ahead
        if place + 1 < len(tasks):
            ahead = score(*tasks[place + 1])
        weights = weigh(*task, s)
        if behind is not None:
            blend(*behind)
        behind = (*task, weights)
    blend(*behind)


def attend(labels, x, chunks, share):
    nseq, _, head_size = x.shape
    rows = nseq * share
    rate = math.log2(math.e) / math.sqrt(head_size)
    whole = pl.BlockSpec(memory_space=pltpu.VMEM)
    return pl.pallas_call(
        functools.partial(attend_kernel, share=share, rate=rate),
        out_shape=jax.ShapeDtypeStruct((nseq, chunks * share, head_size), jnp.bfloat16),
        in_specs=[whole, whole],
        out_specs=whole,
        scratch_shapes=[pltpu.VMEM((chunks, rows, head_size + 128), jnp.bfloat16)],
        compiler_params=pltpu.CompilerParams(vmem_limit_bytes=40 << 20),
        name="attend",
    )(labels, x)


def cross_kernel(x_ref, lab_ref, o_ref):
    tok, heads, width = x_ref.shape
    nseq = o_ref.shape[0]
    half = nseq // 2
    pad = jnp.zeros((4, 128), jnp.float32)
    for dst in range(nseq):
        other = dst ^ half
        labels = [lab_ref[2 * dst : 2 * dst + 2, :], lab_ref[2 * other : 2 * other + 2, :]]
        labels = [piece.astype(jnp.float32) for piece in labels]
        o_ref[dst, 4 * tok : 4 * tok + 8, :] = jnp.concatenate(labels + [pad], axis=0).astype(
            jnp.bfloat16
        )
    for first in range(0, tok, 32):
        for part in range(3):
            low = heads // 2 if part == 2 else 0
            high = heads // 2 if part == 0 else heads
            piece = x_ref[first : first + 32, low:high, part * 128 : (part + 1) * 128]
            turned = jnp.swapaxes(piece.astype(jnp.float32), 0, 1).astype(jnp.bfloat16)
            for head in range(low, high):
                row = (head % 2 + (0 if part == 1 else 2)) * tok + first
                o_ref[head // 2, row : row + 32, :] = turned[head - low]


def near_kernel(me_ref, x_ref, *rest):
    near_refs, turn_ref = rest[:-1], rest[-1]
    tok, heads, width = x_ref.shape
    half = len(near_refs)
    me = me_ref[0]
    for first in range(0, tok, 32):
        piece = x_ref[first : first + 32].astype(jnp.float32)
        turned = jnp.swapaxes(piece, 0, 1).astype(jnp.bfloat16)
        for head in range(heads):
            for part in range(3):
                turn_ref[head, part, first : first + 32, :] = turned[
                    head, :, part * 128 : (part + 1) * 128
                ]
    near_part = jnp.where(me >= half, 0, 2)
    for k, near_ref in enumerate(near_refs):
        dst = me ^ k
        other = dst ^ half
        for j in range(2):
            near_ref[j * tok : (j + 1) * tok, :] = turn_ref[2 * dst + j, near_part]
            for part in range(3):
                row = (2 + 2 * part + j) * tok
                near_ref[row : row + tok, :] = turn_ref[2 * other + j, part]


def spread(me, qkv, labels, nseq):
    tok, heads, width = qkv.shape
    whole = pl.BlockSpec(memory_space=pltpu.VMEM)
    params = pltpu.CompilerParams(vmem_limit_bytes=SPREAD_MB << 20)
    cross = pl.pallas_call(
        cross_kernel,
        out_shape=jax.ShapeDtypeStruct((nseq, 4 * tok + 8, 128), jnp.bfloat16),
        in_specs=[whole, whole],
        out_specs=whole,
        compiler_params=params,
        name="cross",
    )(qkv, labels)
    near = jax.ShapeDtypeStruct((8 * tok, 128), jnp.bfloat16)
    near = pl.pallas_call(
        near_kernel,
        out_shape=[near] * (nseq // 2),
        in_specs=[pl.BlockSpec(memory_space=pltpu.SMEM), whole],
        out_specs=[whole] * (nseq // 2),
        scratch_shapes=[pltpu.VMEM((heads, 3, tok, 128), jnp.bfloat16)],
        compiler_params=params,
        name="near",
    )(me, qkv)
    return cross, near


def run_tasks(tasks, score, weigh, blend):
    ahead = score(*tasks[0])
    behind = None
    for place, task in enumerate(tasks):
        s = ahead
        if place + 1 < len(tasks):
            ahead = score(*tasks[place + 1])
        found = weigh(*task, s)
        if behind is not None:
            blend(*behind)
        behind = (*task, *found)
    blend(*behind)


def dot_t(a, b):
    return lax.dot_general(a, b, (((1,), (1,)), ((), ())), preferred_element_type=jnp.float32)


def soften(s, lab_q, lab_k, diagonal, rate):
    pieces = []
    for i, lab in enumerate(lab_k):
        keep = lab_q == lab
        if diagonal is not None and i * 128 >= diagonal:
            lanes = lax.broadcasted_iota(jnp.int32, (QB, 128), 1) + (i * 128 - diagonal)
            keep = keep & (lanes <= lax.broadcasted_iota(jnp.int32, (QB, 128), 0))
        pieces.append(jnp.where(keep, s[:, i * 128 : (i + 1) * 128], NEG))
    peak = functools.reduce(jnp.maximum, pieces)
    peak = jnp.broadcast_to(jnp.max(peak, axis=1, keepdims=True), (QB, 128))
    pieces = [jnp.exp2((piece - peak) * rate).astype(jnp.bfloat16) for piece in pieces]
    return jnp.concatenate(pieces, axis=1), peak


def columns(rows):
    return jnp.concatenate(
        [jnp.transpose(jnp.broadcast_to(row, (128, 128))) for row in rows], axis=0
    )


def three_parts(stats):
    rows = []
    for row in stats:
        for _ in range(3):
            part = row.astype(jnp.bfloat16).astype(jnp.float32)
            rows.append(part)
            row = row - part
    rows.append(jnp.zeros((8 - len(rows), 128), jnp.float32))
    return jnp.concatenate(rows, axis=0).astype(jnp.bfloat16)


def own_kernel(me_ref, lab_ref, x_ref, *rest, tok, rate):
    nseq = x_ref.shape[0]
    half = nseq // 2
    span = half * tok
    near_refs, o_ref = rest[:half], rest[half]
    q_ref, v_ref, num_ref, sum_ref, peak_ref, stat_ref = rest[half + 1 :]
    me = me_ref[0]
    upper = me >= half
    up = upper.astype(jnp.int32)
    for j in range(2):
        for slot in range(2):
            v_ref[j, slot, :, 128:] = jnp.ones((span, 128), jnp.bfloat16)

    @pl.when(upper)
    def _():
        for j in range(2):
            for k, near_ref in enumerate(near_refs):
                place = pl.multiple_of(((me ^ k) % half) * tok, tok)
                q_ref[j, 1, pl.ds(place, tok), :] = near_ref[j * tok : (j + 1) * tok, :]
            for slot in range(2):
                v_ref[j, slot, :, :128] = x_ref[
                    slot * half : (slot + 1) * half, (2 + j) * tok : (3 + j) * tok, :
                ].reshape(span, 128)

    @pl.when(jnp.logical_not(upper))
    def _():
        for j in range(2):
            for k, near_ref in enumerate(near_refs):
                place = pl.multiple_of(((me ^ k) % half) * tok, tok)
                v_ref[j, 0, pl.ds(place, tok), :128] = near_ref[j * tok : (j + 1) * tok, :]
            for slot in range(2):
                q_ref[j, slot] = x_ref[
                    slot * half : (slot + 1) * half, (2 + j) * tok : (3 + j) * tok, :
                ].reshape(span, 128)

    def keys(j, first, count):
        return x_ref[pl.ds(first, count), j * tok : (j + 1) * tok, :].reshape(count * tok, 128)

    def lab_of(j, first, count):
        return [lab_ref[j, pl.ds(first + i, 1), :] for i in range(count)]

    per = QB // tok

    def score(cross, j, block):
        rows = pl.ds(block * QB, QB)
        if cross:
            return dot_t(q_ref[j, 1, rows, :], keys(j, 0, half))
        return dot_t(q_ref[j, up, rows, :], keys(j, up * half, (block + 1) * per))

    def weigh(cross, j, block, s):
        if cross:
            lab_q = columns(lab_of(j, half + block * per, per))
            return soften(s, lab_q, lab_of(j, 0, half), None, rate)
        lab_q = columns(lab_of(j, up * half + block * per, per))
        lab_k = lab_of(j, up * half, (block + 1) * per)
        return soften(s, lab_q, lab_k, block * QB, rate)

    def blend(cross, j, block, weights, peak):
        rows = pl.ds(block * QB, QB)
        if cross:
            both = jnp.dot(weights, v_ref[j, 0], preferred_element_type=jnp.float32)
            num, total = both[:, :128], both[:, 128:]
            num_ref[j, rows, :] = num
            sum_ref[j, rows, :] = total
            peak_ref[j, rows, :] = peak
            lse = peak * rate + jnp.log2(total)
            for i in range(per):
                turned = jnp.transpose(lse[i * tok : (i + 1) * tok, :])
                stat_ref[j, block * per + i : block * per + i + 1, :] = turned[:1, :]
            out = num / total
            first = (1 - up) * half + block * per
        else:
            both = jnp.dot(
                weights, v_ref[j, up, : (block + 1) * QB, :], preferred_element_type=jnp.float32
            )
            far = jnp.where(upper, peak_ref[j, rows, :], NEG)
            top = jnp.maximum(peak, far)
            here = jnp.exp2((peak - top) * rate)
            there = jnp.exp2((far - top) * rate)
            num = both[:, :128] * here + num_ref[j, rows, :] * there
            out = num / (both[:, 128:] * here + sum_ref[j, rows, :] * there)
            first = up * half + block * per
        o_ref[pl.ds(first, per), j * tok : (j + 1) * tok, :] = out.astype(jnp.bfloat16).reshape(
            per, tok, 128
        )

    blocks = span // QB
    tasks = [(True, j, block) for block in range(blocks) for j in range(2)]
    tasks += [
        (False, j, block if j == 0 else blocks - 1 - block)
        for block in range(blocks)
        for j in range(2)
    ]
    run_tasks(tasks, score, weigh, blend)
    for i in range(half):
        stats = three_parts([stat_ref[j, i : i + 1, :] for j in range(2)])
        o_ref[(1 - up) * half + i, 2 * tok : 2 * tok + 8, :] = stats
        o_ref[up * half + i, 2 * tok : 2 * tok + 8, :] = jnp.zeros((8, 128), jnp.bfloat16)


def own(me, labels, x, near, tok, rate):
    nseq = x.shape[0]
    half = nseq // 2
    span = half * tok
    whole = pl.BlockSpec(memory_space=pltpu.VMEM)
    return pl.pallas_call(
        functools.partial(own_kernel, tok=tok, rate=rate),
        out_shape=jax.ShapeDtypeStruct((nseq, 2 * tok + 8, 128), jnp.bfloat16),
        in_specs=[pl.BlockSpec(memory_space=pltpu.SMEM)] + [whole] * (2 + half),
        out_specs=whole,
        scratch_shapes=[
            pltpu.VMEM((2, 2, span, 128), jnp.bfloat16),
            pltpu.VMEM((2, 2, span, 256), jnp.bfloat16),
            pltpu.VMEM((2, span, 128), jnp.float32),
            pltpu.VMEM((2, span, 128), jnp.float32),
            pltpu.VMEM((2, span, 128), jnp.float32),
            pltpu.VMEM((2, half, 128), jnp.float32),
        ],
        compiler_params=pltpu.CompilerParams(vmem_limit_bytes=20 << 20),
        name="own",
    )(me, labels, x, *near)


def partner_kernel(me_ref, lab_ref, *rest, tok, rate):
    half = (len(rest) - 5) // 2
    near_refs, o_refs = rest[:half], rest[half : 2 * half]
    q_ref, k_ref, v_ref, out_ref, stat_ref = rest[2 * half :]
    span = half * tok
    me = me_ref[0]
    up = (me >= half).astype(jnp.int32)
    for j in range(2):
        v_ref[j, :, 128:] = jnp.ones((span, 128), jnp.bfloat16)
        for k, near_ref in enumerate(near_refs):
            place = pl.ds(pl.multiple_of(((me ^ k) % half) * tok, tok), tok)
            q_ref[j, place, :] = near_ref[(2 + j) * tok : (3 + j) * tok, :]
            k_ref[j, place, :] = near_ref[(4 + j) * tok : (5 + j) * tok, :]
            v_ref[j, place, :128] = near_ref[(6 + j) * tok : (7 + j) * tok, :]

    def lab_of(j, first, count):
        return [lab_ref[2 + j, pl.ds(up * half + first + i, 1), :] for i in range(count)]

    per = QB // tok

    def score(j, block):
        return dot_t(q_ref[j, pl.ds(block * QB, QB), :], k_ref[j, : (block + 1) * QB, :])

    def weigh(j, block, s):
        lab_q = columns(lab_of(j, block * per, per))
        return soften(s, lab_q, lab_of(j, 0, (block + 1) * per), block * QB, rate)

    def blend(j, block, weights, peak):
        both = jnp.dot(
            weights, v_ref[j, : (block + 1) * QB, :], preferred_element_type=jnp.float32
        )
        num, total = both[:, :128], both[:, 128:]
        lse = peak * rate + jnp.log2(total)
        out = (num / total).astype(jnp.bfloat16)
        for i in range(per):
            turned = jnp.transpose(lse[i * tok : (i + 1) * tok, :])
            stat_ref[j, block * per + i : block * per + i + 1, :] = turned[:1, :]
            out_ref[block * per + i, j * tok : (j + 1) * tok, :] = out[i * tok : (i + 1) * tok, :]

    blocks = span // QB
    tasks = [
        (j, block if j == 0 else blocks - 1 - block) for block in range(blocks) for j in range(2)
    ]
    run_tasks(tasks, score, weigh, blend)
    for i in range(half):
        stats = three_parts([stat_ref[j, i : i + 1, :] for j in range(2)])
        out_ref[i, 2 * tok : 2 * tok + 8, :] = stats
    for k, o_ref in enumerate(o_refs):
        o_ref[...] = out_ref[(me ^ k) % half]


def partner(me, labels, near, tok, rate):
    half = len(near)
    span = half * tok
    whole = pl.BlockSpec(memory_space=pltpu.VMEM)
    return pl.pallas_call(
        functools.partial(partner_kernel, tok=tok, rate=rate),
        out_shape=[jax.ShapeDtypeStruct((2 * tok + 8, 128), jnp.bfloat16)] * half,
        in_specs=[pl.BlockSpec(memory_space=pltpu.SMEM)] + [whole] * (1 + half),
        out_specs=[whole] * half,
        scratch_shapes=[
            pltpu.VMEM((2, span, 128), jnp.bfloat16),
            pltpu.VMEM((2, span, 128), jnp.bfloat16),
            pltpu.VMEM((2, span, 256), jnp.bfloat16),
            pltpu.VMEM((half, 2 * tok + 8, 128), jnp.bfloat16),
            pltpu.VMEM((2, half, 128), jnp.float32),
        ],
        compiler_params=pltpu.CompilerParams(vmem_limit_bytes=16 << 20),
        name="partner",
    )(me, labels, *near)


def merge_kernel(me_ref, x_ref, *rest, tok):
    nseq = x_ref.shape[0]
    half = nseq // 2
    near_refs, o_ref, head_ref = rest[:half], rest[half], rest[half + 1]
    me = me_ref[0]
    upper = me >= half
    up = upper.astype(jnp.int32)
    down = 1 - up
    heads = 2 * nseq
    for i in range(half):
        for j in range(2):
            head_ref[up * (heads // 2) + 2 * i + j] = x_ref[
                up * half + i, j * tok : (j + 1) * tok, :
            ].astype(jnp.float32)
    for k, near_ref in enumerate(near_refs):
        place = (me ^ k) % half
        far_stats = x_ref[down * half + place, 2 * tok : 2 * tok + 8, :].astype(jnp.float32)
        near_stats = near_ref[2 * tok : 2 * tok + 8, :].astype(jnp.float32)
        for j in range(2):
            near_lse = sum(near_stats[3 * j + c : 3 * j + c + 1, :] for c in range(3))
            far_lse = sum(far_stats[3 * j + c : 3 * j + c + 1, :] for c in range(3))
            weight = jnp.where(upper, 1.0 / (1.0 + jnp.exp2(near_lse - far_lse)), 0.0)
            weight = jnp.transpose(jnp.broadcast_to(weight, (128, tok)))
            far = x_ref[down * half + place, j * tok : (j + 1) * tok, :].astype(jnp.float32)
            near = near_ref[j * tok : (j + 1) * tok, :].astype(jnp.float32)
            head_ref[down * (heads // 2) + 2 * place + j] = near + (far - near) * weight
    for first in range(0, tok, 32):
        piece = head_ref[:, first : first + 32, :]
        o_ref[first : first + 32] = jnp.swapaxes(piece, 0, 1).astype(jnp.bfloat16)


def merge(me, x, near, tok):
    nseq = x.shape[0]
    whole = pl.BlockSpec(memory_space=pltpu.VMEM)
    return pl.pallas_call(
        functools.partial(merge_kernel, tok=tok),
        out_shape=jax.ShapeDtypeStruct((tok, 2 * nseq, 128), jnp.bfloat16),
        in_specs=[pl.BlockSpec(memory_space=pltpu.SMEM)] + [whole] * (1 + nseq // 2),
        out_specs=whole,
        scratch_shapes=[pltpu.VMEM((2 * nseq, tok, 128), jnp.float32)],
        compiler_params=pltpu.CompilerParams(vmem_limit_bytes=12 << 20),
        name="merge",
    )(me, x, *near)


def two_halves(qkv, labels):
    tok, heads, width = qkv.shape
    nseq = lax.axis_size("seq")
    rate = math.log2(math.e) / math.sqrt(width // 3)
    me = lax.axis_index("seq").astype(jnp.int32).reshape(1)

    def exchange(x):
        return lax.all_to_all(x, "seq", split_axis=0, concat_axis=0, tiled=True)

    def swap(blocks):
        moved = list(blocks)
        for k in reversed(range(1, len(blocks))):
            moved[k] = lax.ppermute(blocks[k], "seq", [(i, i ^ k) for i in range(nseq)])
        return moved

    cross, near = spread(me, qkv, labels, nseq)
    near = swap(near)
    cross = exchange(cross)
    labels = jnp.transpose(cross[:, 4 * tok : 4 * tok + 4, :].astype(jnp.int32), (1, 0, 2))
    back = exchange(own(me, labels, cross, near, tok, rate))
    near_back = swap(partner(me, labels, near, tok, rate))
    return merge(me, back, near_back, tok)


def local(qkv, routes):
    tok, heads, width = qkv.shape
    head_size = width // 3
    nseq = lax.axis_size("seq")
    clusters = nseq * tok // CLEN
    pairs_dev = heads * tok // CLEN
    chunks = max(1, pairs_dev // clusters)
    split = max(1, clusters // pairs_dev)
    share = tok // split

    def exchange(x):
        return lax.all_to_all(x, "seq", split_axis=0, concat_axis=0, tiled=True)

    labels = jnp.transpose(routes)
    paired = nseq & (nseq - 1) == 0 and nseq * tok // 2 % QB == 0
    if split == 1 and chunks == 2 and paired and tok == 128 and head_size == 128:
        return two_halves(qkv, labels)
    if split == 1:
        rows = exchange(pack(qkv, labels, chunks))
    else:
        group = labels // pairs_dev
        member = group[:, :, None] == jnp.arange(split, dtype=jnp.int32)[None, None, :]
        rank = jnp.cumsum(member.astype(jnp.int32), axis=1) - 1
        slot = group * share + jnp.sum(jnp.where(member, rank, 0), axis=2)
        pick = slot[:, None, :] == jnp.arange(tok, dtype=jnp.int32)[None, :, None]
        moved = jnp.einsum(
            "hst,thd->hsd", pick.astype(jnp.bfloat16), qkv, preferred_element_type=jnp.float32
        ).astype(jnp.bfloat16)
        labels = jnp.sum(jnp.where(pick, labels[:, None, :], 0), axis=2)
        moved = moved.reshape(nseq, share, 3, head_size)
        moved = jnp.transpose(moved, (0, 2, 1, 3)).reshape(nseq, 3 * share, head_size)
        extra = labels.reshape(nseq, 1, share).astype(jnp.bfloat16)
        extra = jnp.pad(extra, ((0, 0), (0, 7), (0, head_size - share)))
        rows = exchange(jnp.concatenate([moved, extra], axis=1))
    first = chunks * 3 * share
    arrived = rows[:, first : first + chunks, :share].astype(jnp.int32)
    arrived = jnp.transpose(arrived, (1, 0, 2)).reshape(chunks, nseq * share // 128, 128)
    back = exchange(attend(arrived, rows, chunks, share)).reshape(heads, tok, head_size)
    if split > 1:
        back = jnp.einsum(
            "hst,hsd->htd", pick.astype(jnp.bfloat16), back, preferred_element_type=jnp.float32
        ).astype(jnp.bfloat16)
    return unpack(back)


def solution(mesh):
    placed = (P(("groups", "seq"), None, None), P(("groups", "seq"), None))
    return jax.shard_map(
        local,
        mesh=mesh,
        in_specs=placed,
        out_specs=P(("groups", "seq"), None, None),
        check_vma=False,
    )
```

```python
import functools
import math

import jax
import jax.numpy as jnp
from jax import lax
from jax.experimental import pallas as pl
from jax.experimental.pallas import tpu as pltpu
from jax.sharding import PartitionSpec as P

CLEN = 1024
QB = 256
STEP = 64
NEG = -1e30


def pack_kernel(x_ref, lab_ref, o_ref, *, chunks):
    tok, heads, width = x_ref.shape
    parts = width // 128
    pad = jnp.zeros((8 - chunks, 128), jnp.float32)
    for dst in range(heads // chunks):
        labels = lab_ref[dst * chunks : (dst + 1) * chunks, :]
        o_ref[dst, pl.ds(chunks * parts * tok, 8), :] = jnp.concatenate(
            [labels.astype(jnp.float32), pad], axis=0
        ).astype(jnp.bfloat16)
    for first in range(0, tok, 32):
        piece = x_ref[first : first + 32].astype(jnp.float32)
        turned = jnp.swapaxes(piece, 0, 1).astype(jnp.bfloat16)
        for head in range(heads):
            for part in range(parts):
                row = (head % chunks * parts + part) * tok + first
                o_ref[head // chunks, row : row + 32, :] = turned[
                    head, :, part * 128 : (part + 1) * 128
                ]


def pack(qkv, labels, chunks):
    tok, heads, width = qkv.shape
    rows = chunks * (width // 128) * tok + 8
    whole = pl.BlockSpec(memory_space=pltpu.VMEM)
    return pl.pallas_call(
        functools.partial(pack_kernel, chunks=chunks),
        out_shape=jax.ShapeDtypeStruct((heads // chunks, rows, 128), jnp.bfloat16),
        in_specs=[whole, whole],
        out_specs=whole,
        compiler_params=pltpu.CompilerParams(vmem_limit_bytes=32 << 20),
        name="pack",
    )(qkv, labels)


def unpack_kernel(x_ref, o_ref):
    o_ref[...] = jnp.swapaxes(x_ref[...].astype(jnp.float32), 0, 1).astype(jnp.bfloat16)


def unpack(back):
    heads, tok, head_size = back.shape
    return pl.pallas_call(
        unpack_kernel,
        out_shape=jax.ShapeDtypeStruct((tok, heads, head_size), jnp.bfloat16),
        grid=(tok // STEP,),
        in_specs=[pl.BlockSpec((heads, STEP, head_size), lambda i: (0, i, 0))],
        out_specs=pl.BlockSpec((STEP, heads, head_size), lambda i: (i, 0, 0)),
        name="unpack",
    )(back)


def attend_kernel(lab_ref, x_ref, o_ref, v_ref, *, share, rate):
    nseq, _, head_size = x_ref.shape
    chunks = lab_ref.shape[0]
    rows = nseq * share
    ramp = lax.broadcasted_iota(jnp.int32, (QB, QB), 1) <= lax.broadcasted_iota(
        jnp.int32, (QB, QB), 0
    )

    def rows_of(chunk, part, first, count):
        base = (chunk * 3 + part) * share
        piece = x_ref[first // share : (first + count) // share, base : base + share, :]
        return piece.reshape(count, head_size)

    for chunk in range(chunks):
        v_ref[chunk, :, :head_size] = rows_of(chunk, 2, 0, rows)
        v_ref[chunk, :, head_size:] = jnp.ones((rows, 128), jnp.bfloat16)

    def score(chunk, block):
        return lax.dot_general(
            rows_of(chunk, 0, block * QB, QB),
            rows_of(chunk, 1, 0, (block + 1) * QB),
            (((1,), (1,)), ((), ())),
            preferred_element_type=jnp.float32,
        )

    def weigh(chunk, block, s):
        row0 = block * QB
        stop = row0 + QB
        lab_q = jnp.concatenate(
            [
                jnp.transpose(jnp.broadcast_to(lab_ref[chunk, i : i + 1, :], (128, 128)))
                for i in range(row0 // 128, stop // 128)
            ],
            axis=0,
        )
        pieces = []
        for i in range(stop // 128):
            keep = lab_q == lab_ref[chunk, i : i + 1, :]
            if i * 128 >= row0:
                keep = keep & ramp[:, i * 128 - row0 : i * 128 - row0 + 128]
            pieces.append(jnp.where(keep, s[:, i * 128 : (i + 1) * 128], NEG))
        peak = functools.reduce(jnp.maximum, pieces)
        peak = jnp.broadcast_to(jnp.max(peak, axis=1, keepdims=True), (QB, 128))
        pieces = [jnp.exp2((piece - peak) * rate).astype(jnp.bfloat16) for piece in pieces]
        return jnp.concatenate(pieces, axis=1)

    def blend(chunk, block, weights):
        row0 = block * QB
        stop = row0 + QB
        both = jnp.dot(weights, v_ref[chunk, :stop, :], preferred_element_type=jnp.float32)
        out = both[:, :head_size] / both[:, head_size:]
        o_ref[row0 // share : stop // share, chunk * share : (chunk + 1) * share] = out.astype(
            jnp.bfloat16
        ).reshape(QB // share, share, head_size)

    blocks = rows // QB
    tasks = [
        (chunk, step if chunk % 2 == 0 else blocks - 1 - step)
        for step in range(blocks)
        for chunk in range(chunks)
    ]
    ahead = score(*tasks[0])
    behind = None
    for place, task in enumerate(tasks):
        s = ahead
        if place + 1 < len(tasks):
            ahead = score(*tasks[place + 1])
        weights = weigh(*task, s)
        if behind is not None:
            blend(*behind)
        behind = (*task, weights)
    blend(*behind)


def attend(labels, x, chunks, share):
    nseq, _, head_size = x.shape
    rows = nseq * share
    rate = math.log2(math.e) / math.sqrt(head_size)
    whole = pl.BlockSpec(memory_space=pltpu.VMEM)
    return pl.pallas_call(
        functools.partial(attend_kernel, share=share, rate=rate),
        out_shape=jax.ShapeDtypeStruct((nseq, chunks * share, head_size), jnp.bfloat16),
        in_specs=[whole, whole],
        out_specs=whole,
        scratch_shapes=[pltpu.VMEM((chunks, rows, head_size + 128), jnp.bfloat16)],
        compiler_params=pltpu.CompilerParams(vmem_limit_bytes=40 << 20),
        name="attend",
    )(labels, x)


def cross_kernel(me_ref, x_ref, lab_ref, o_ref):
    tok, heads, width = x_ref.shape
    nseq = o_ref.shape[0]
    half = nseq // 2
    lane = pl.multiple_of(jnp.where(me_ref[0] >= half, 0, 128), 128)
    pad = jnp.zeros((4, 128), jnp.float32)
    for dst in range(nseq):
        other = dst ^ half
        labels = [lab_ref[2 * dst : 2 * dst + 2, :], lab_ref[2 * other : 2 * other + 2, :]]
        labels = [piece.astype(jnp.float32) for piece in labels]
        o_ref[dst, 4 * tok : 4 * tok + 8, :] = jnp.concatenate(labels + [pad], axis=0).astype(
            jnp.bfloat16
        )
    for first in range(0, tok, 32):
        piece = x_ref[first : first + 32, :, pl.ds(lane, 256)].astype(jnp.float32)
        turned = jnp.swapaxes(piece, 0, 1).astype(jnp.bfloat16)
        for head in range(heads):
            for part in range(2):
                row = (2 * part + head % 2) * tok + first
                o_ref[head // 2, row : row + 32, :] = turned[
                    head, :, part * 128 : (part + 1) * 128
                ]


def near_kernel(me_ref, x_ref, *rest):
    near_refs, turn_ref = rest[:-1], rest[-1]
    tok, heads, width = x_ref.shape
    half = len(near_refs)
    me = me_ref[0]
    for first in range(0, tok, 32):
        piece = x_ref[first : first + 32].astype(jnp.float32)
        turned = jnp.swapaxes(piece, 0, 1).astype(jnp.bfloat16)
        for head in range(heads):
            for part in range(3):
                turn_ref[head, part, first : first + 32, :] = turned[
                    head, :, part * 128 : (part + 1) * 128
                ]
    near_part = jnp.where(me >= half, 2, 0)
    for k, near_ref in enumerate(near_refs):
        dst = me ^ k
        other = dst ^ half
        for j in range(2):
            near_ref[j * tok : (j + 1) * tok, :] = turn_ref[2 * dst + j, near_part]
            for part in range(3):
                row = (2 + 2 * part + j) * tok
                near_ref[row : row + tok, :] = turn_ref[2 * other + j, part]


def spread(me, qkv, labels, nseq):
    tok, heads, width = qkv.shape
    whole = pl.BlockSpec(memory_space=pltpu.VMEM)
    scalar = pl.BlockSpec(memory_space=pltpu.SMEM)
    params = pltpu.CompilerParams(vmem_limit_bytes=12 << 20)
    cross = pl.pallas_call(
        cross_kernel,
        out_shape=jax.ShapeDtypeStruct((nseq, 4 * tok + 8, 128), jnp.bfloat16),
        in_specs=[scalar, whole, whole],
        out_specs=whole,
        compiler_params=params,
        name="cross",
    )(me, qkv, labels)
    near = pl.pallas_call(
        near_kernel,
        out_shape=[jax.ShapeDtypeStruct((8 * tok, 128), jnp.bfloat16)] * (nseq // 2),
        in_specs=[scalar, whole],
        out_specs=[whole] * (nseq // 2),
        scratch_shapes=[pltpu.VMEM((heads, 3, tok, 128), jnp.bfloat16)],
        compiler_params=params,
        name="near",
    )(me, qkv)
    return cross, near


def run_tasks(tasks, score, weigh, blend):
    ahead = score(*tasks[0])
    behind = None
    for place, task in enumerate(tasks):
        s = ahead
        if place + 1 < len(tasks):
            ahead = score(*tasks[place + 1])
        found = weigh(*task, s)
        if behind is not None:
            blend(*behind)
        behind = (*task, *found)
    blend(*behind)


def dot_t(a, b):
    return lax.dot_general(a, b, (((1,), (1,)), ((), ())), preferred_element_type=jnp.float32)


def soften(s, lab_q, lab_k, diagonal, rate):
    pieces = []
    for i, lab in enumerate(lab_k):
        keep = lab_q == lab
        if diagonal is not None and i * 128 >= diagonal:
            lanes = lax.broadcasted_iota(jnp.int32, (QB, 128), 1) + (i * 128 - diagonal)
            keep = keep & (lanes <= lax.broadcasted_iota(jnp.int32, (QB, 128), 0))
        pieces.append(jnp.where(keep, s[:, i * 128 : (i + 1) * 128], NEG))
    peak = functools.reduce(jnp.maximum, pieces)
    peak = jnp.broadcast_to(jnp.max(peak, axis=1, keepdims=True), (QB, 128))
    pieces = [jnp.exp2((piece - peak) * rate).astype(jnp.bfloat16) for piece in pieces]
    return jnp.concatenate(pieces, axis=1), peak


def columns(rows):
    return jnp.concatenate(
        [jnp.transpose(jnp.broadcast_to(row, (128, 128))) for row in rows], axis=0
    )


def three_parts(stats):
    rows = []
    for row in stats:
        for _ in range(3):
            part = row.astype(jnp.bfloat16).astype(jnp.float32)
            rows.append(part)
            row = row - part
    rows.append(jnp.zeros((8 - len(rows), 128), jnp.float32))
    return jnp.concatenate(rows, axis=0).astype(jnp.bfloat16)


def finish(both, peak, rate, tok):
    num, total = both[:, :128], both[:, 128:]
    lse = peak * rate + jnp.log2(total)
    rows = [jnp.transpose(lse[i : i + tok, :])[:1, :] for i in range(0, QB, tok)]
    return num / total, rows


def far_kernel(lab_ref, x_ref, o_ref, stat_ref, v_ref, *, tok, rate):
    nseq = x_ref.shape[0]
    half = nseq // 2
    span = half * tok
    per = QB // tok
    for j in range(2):
        v_ref[j, :, :128] = x_ref[:half, (2 + j) * tok : (3 + j) * tok, :].reshape(span, 128)
        v_ref[j, :, 128:] = jnp.ones((span, 128), jnp.bfloat16)

    def score(j, block):
        first = half + block * per
        q = x_ref[first : first + per, j * tok : (j + 1) * tok, :].reshape(QB, 128)
        return dot_t(q, x_ref[:half, j * tok : (j + 1) * tok, :].reshape(span, 128))

    def weigh(j, block, s):
        first = half + block * per
        lab_q = columns([lab_ref[j, first + i : first + i + 1, :] for i in range(per)])
        return soften(s, lab_q, [lab_ref[j, i : i + 1, :] for i in range(half)], None, rate)

    def blend(j, block, weights, peak):
        both = jnp.dot(weights, v_ref[j], preferred_element_type=jnp.float32)
        out, rows = finish(both, peak, rate, tok)
        for i, row in enumerate(rows):
            stat_ref[j, block * per + i : block * per + i + 1, :] = row
        o_ref[j, block * QB : (block + 1) * QB, :] = out

    run_tasks([(j, block) for block in range(span // QB) for j in range(2)], score, weigh, blend)


def far_of(labels, x, tok, rate):
    half = x.shape[0] // 2
    whole = pl.BlockSpec(memory_space=pltpu.VMEM)
    return pl.pallas_call(
        functools.partial(far_kernel, tok=tok, rate=rate),
        out_shape=[
            jax.ShapeDtypeStruct((2, half * tok, 128), jnp.float32),
            jax.ShapeDtypeStruct((2, half, 128), jnp.float32),
        ],
        in_specs=[whole, whole],
        out_specs=[whole, whole],
        scratch_shapes=[pltpu.VMEM((2, half * tok, 256), jnp.bfloat16)],
        compiler_params=pltpu.CompilerParams(vmem_limit_bytes=16 << 20),
        name="far",
    )(labels, x)


def own_kernel(me_ref, lab_ref, x_ref, far_ref, far_stat_ref, *rest, tok, rate):
    half = x_ref.shape[0] // 2
    near_refs, o_ref = rest[:half], rest[half]
    q_ref, k_ref, v_ref = rest[half + 1 :]
    span = half * tok
    per = QB // tok
    me = me_ref[0]
    upper = me >= half
    up = upper.astype(jnp.int32)
    places = [pl.ds(pl.multiple_of(((me ^ k) % half) * tok, tok), tok) for k in range(half)]

    @pl.when(upper)
    def _():
        for j in range(2):
            q_ref[j] = x_ref[half:, j * tok : (j + 1) * tok, :].reshape(span, 128)
            k_ref[j] = x_ref[half:, (2 + j) * tok : (3 + j) * tok, :].reshape(span, 128)
            for place, near_ref in zip(places, near_refs):
                v_ref[j, place, :128] = near_ref[j * tok : (j + 1) * tok, :]

    @pl.when(jnp.logical_not(upper))
    def _():
        for j in range(2):
            k_ref[j] = x_ref[:half, j * tok : (j + 1) * tok, :].reshape(span, 128)
            v_ref[j, :, :128] = x_ref[:half, (2 + j) * tok : (3 + j) * tok, :].reshape(span, 128)
            for place, near_ref in zip(places, near_refs):
                q_ref[j, place, :] = near_ref[j * tok : (j + 1) * tok, :]

    for j in range(2):
        v_ref[j, :, 128:] = jnp.ones((span, 128), jnp.bfloat16)

    def lab_of(j, first, count):
        return [lab_ref[j, pl.ds(up * half + first + i, 1), :] for i in range(count)]

    def score(j, block):
        return dot_t(q_ref[j, block * QB : (block + 1) * QB, :], k_ref[j, : (block + 1) * QB, :])

    def weigh(j, block, s):
        lab_q = columns(lab_of(j, block * per, per))
        return soften(s, lab_q, lab_of(j, 0, (block + 1) * per), block * QB, rate)

    def blend(j, block, weights, peak):
        both = jnp.dot(
            weights, v_ref[j, : (block + 1) * QB, :], preferred_element_type=jnp.float32
        )
        total = both[:, 128:]
        near = both[:, :128] / total
        rows = [
            far_stat_ref[j, i : i + 1, :] for i in range(block * per, (block + 1) * per)
        ]
        gap = peak * rate + jnp.log2(total) - columns(rows)
        weight = jnp.where(upper, 1.0 / (1.0 + jnp.exp2(gap)), 0.0)
        far = far_ref[j, block * QB : (block + 1) * QB, :]
        out = near + (far - near) * weight
        o_ref[pl.ds(up * half + block * per, per), j * tok : (j + 1) * tok, :] = out.astype(
            jnp.bfloat16
        ).reshape(per, tok, 128)
        o_ref[pl.ds((1 - up) * half + block * per, per), j * tok : (j + 1) * tok, :] = far.astype(
            jnp.bfloat16
        ).reshape(per, tok, 128)

    blocks = span // QB
    tasks = [
        (j, block if j == 0 else blocks - 1 - block) for block in range(blocks) for j in range(2)
    ]
    run_tasks(tasks, score, weigh, blend)
    for i in range(half):
        stats = three_parts([far_stat_ref[j, i : i + 1, :] for j in range(2)])
        o_ref[(1 - up) * half + i, 2 * tok : 2 * tok + 8, :] = stats
        o_ref[up * half + i, 2 * tok : 2 * tok + 8, :] = jnp.zeros((8, 128), jnp.bfloat16)


def own(me, labels, x, far, near, tok, rate):
    nseq = x.shape[0]
    half = nseq // 2
    span = half * tok
    whole = pl.BlockSpec(memory_space=pltpu.VMEM)
    return pl.pallas_call(
        functools.partial(own_kernel, tok=tok, rate=rate),
        out_shape=jax.ShapeDtypeStruct((nseq, 2 * tok + 8, 128), jnp.bfloat16),
        in_specs=[pl.BlockSpec(memory_space=pltpu.SMEM)] + [whole] * (4 + half),
        out_specs=whole,
        scratch_shapes=[
            pltpu.VMEM((2, span, 128), jnp.bfloat16),
            pltpu.VMEM((2, span, 128), jnp.bfloat16),
            pltpu.VMEM((2, span, 256), jnp.bfloat16),
        ],
        compiler_params=pltpu.CompilerParams(vmem_limit_bytes=16 << 20),
        name="own",
    )(me, labels, x, *far, *near)


def partner_kernel(me_ref, lab_ref, *rest, tok, rate):
    half = (len(rest) - 5) // 2
    near_refs, o_refs = rest[:half], rest[half : 2 * half]
    q_ref, k_ref, v_ref, out_ref, stat_ref = rest[2 * half :]
    span = half * tok
    me = me_ref[0]
    up = (me >= half).astype(jnp.int32)
    for j in range(2):
        v_ref[j, :, 128:] = jnp.ones((span, 128), jnp.bfloat16)
        for k, near_ref in enumerate(near_refs):
            place = pl.ds(pl.multiple_of(((me ^ k) % half) * tok, tok), tok)
            q_ref[j, place, :] = near_ref[(2 + j) * tok : (3 + j) * tok, :]
            k_ref[j, place, :] = near_ref[(4 + j) * tok : (5 + j) * tok, :]
            v_ref[j, place, :128] = near_ref[(6 + j) * tok : (7 + j) * tok, :]

    def lab_of(j, first, count):
        return [lab_ref[2 + j, pl.ds(up * half + first + i, 1), :] for i in range(count)]

    per = QB // tok

    def score(j, block):
        return dot_t(q_ref[j, pl.ds(block * QB, QB), :], k_ref[j, : (block + 1) * QB, :])

    def weigh(j, block, s):
        lab_q = columns(lab_of(j, block * per, per))
        return soften(s, lab_q, lab_of(j, 0, (block + 1) * per), block * QB, rate)

    def blend(j, block, weights, peak):
        both = jnp.dot(
            weights, v_ref[j, : (block + 1) * QB, :], preferred_element_type=jnp.float32
        )
        num, total = both[:, :128], both[:, 128:]
        lse = peak * rate + jnp.log2(total)
        out = (num / total).astype(jnp.bfloat16)
        for i in range(per):
            turned = jnp.transpose(lse[i * tok : (i + 1) * tok, :])
            stat_ref[j, block * per + i : block * per + i + 1, :] = turned[:1, :]
            out_ref[block * per + i, j * tok : (j + 1) * tok, :] = out[i * tok : (i + 1) * tok, :]

    blocks = span // QB
    tasks = [
        (j, block if j == 0 else blocks - 1 - block) for block in range(blocks) for j in range(2)
    ]
    run_tasks(tasks, score, weigh, blend)
    for i in range(half):
        stats = three_parts([stat_ref[j, i : i + 1, :] for j in range(2)])
        out_ref[i, 2 * tok : 2 * tok + 8, :] = stats
    for k, o_ref in enumerate(o_refs):
        o_ref[...] = out_ref[(me ^ k) % half]


def partner(me, labels, near, tok, rate):
    half = len(near)
    span = half * tok
    whole = pl.BlockSpec(memory_space=pltpu.VMEM)
    return pl.pallas_call(
        functools.partial(partner_kernel, tok=tok, rate=rate),
        out_shape=[jax.ShapeDtypeStruct((2 * tok + 8, 128), jnp.bfloat16)] * half,
        in_specs=[pl.BlockSpec(memory_space=pltpu.SMEM)] + [whole] * (1 + half),
        out_specs=[whole] * half,
        scratch_shapes=[
            pltpu.VMEM((2, span, 128), jnp.bfloat16),
            pltpu.VMEM((2, span, 128), jnp.bfloat16),
            pltpu.VMEM((2, span, 256), jnp.bfloat16),
            pltpu.VMEM((half, 2 * tok + 8, 128), jnp.bfloat16),
            pltpu.VMEM((2, half, 128), jnp.float32),
        ],
        compiler_params=pltpu.CompilerParams(vmem_limit_bytes=16 << 20),
        name="partner",
    )(me, labels, *near)


def merge_kernel(me_ref, x_ref, *rest, tok):
    nseq = x_ref.shape[0]
    half = nseq // 2
    near_refs, o_ref, head_ref = rest[:half], rest[half], rest[half + 1]
    me = me_ref[0]
    upper = me >= half
    up = upper.astype(jnp.int32)
    down = 1 - up
    heads = 2 * nseq
    for i in range(half):
        for j in range(2):
            head_ref[up * (heads // 2) + 2 * i + j] = x_ref[
                up * half + i, j * tok : (j + 1) * tok, :
            ].astype(jnp.float32)
    for k, near_ref in enumerate(near_refs):
        place = (me ^ k) % half
        far_stats = x_ref[down * half + place, 2 * tok : 2 * tok + 8, :].astype(jnp.float32)
        near_stats = near_ref[2 * tok : 2 * tok + 8, :].astype(jnp.float32)
        for j in range(2):
            near_lse = sum(near_stats[3 * j + c : 3 * j + c + 1, :] for c in range(3))
            far_lse = sum(far_stats[3 * j + c : 3 * j + c + 1, :] for c in range(3))
            weight = jnp.where(upper, 1.0 / (1.0 + jnp.exp2(near_lse - far_lse)), 0.0)
            weight = jnp.transpose(jnp.broadcast_to(weight, (128, tok)))
            far = x_ref[down * half + place, j * tok : (j + 1) * tok, :].astype(jnp.float32)
            near = near_ref[j * tok : (j + 1) * tok, :].astype(jnp.float32)
            head_ref[down * (heads // 2) + 2 * place + j] = near + (far - near) * weight
    for first in range(0, tok, 32):
        piece = head_ref[:, first : first + 32, :]
        o_ref[first : first + 32] = jnp.swapaxes(piece, 0, 1).astype(jnp.bfloat16)


def merge(me, x, near, tok):
    nseq = x.shape[0]
    whole = pl.BlockSpec(memory_space=pltpu.VMEM)
    return pl.pallas_call(
        functools.partial(merge_kernel, tok=tok),
        out_shape=jax.ShapeDtypeStruct((tok, 2 * nseq, 128), jnp.bfloat16),
        in_specs=[pl.BlockSpec(memory_space=pltpu.SMEM)] + [whole] * (1 + nseq // 2),
        out_specs=whole,
        scratch_shapes=[pltpu.VMEM((2 * nseq, tok, 128), jnp.float32)],
        compiler_params=pltpu.CompilerParams(vmem_limit_bytes=12 << 20),
        name="merge",
    )(me, x, *near)


def two_halves(qkv, labels):
    tok, heads, width = qkv.shape
    nseq = lax.axis_size("seq")
    rate = math.log2(math.e) / math.sqrt(width // 3)
    me = lax.axis_index("seq").astype(jnp.int32).reshape(1)

    def exchange(x):
        return lax.all_to_all(x, "seq", split_axis=0, concat_axis=0, tiled=True)

    def swap(blocks):
        moved = list(blocks)
        for k in reversed(range(1, len(blocks))):
            moved[k] = lax.ppermute(blocks[k], "seq", [(i, i ^ k) for i in range(nseq)])
        return moved

    cross, near = spread(me, qkv, labels, nseq)
    near = swap(near)
    cross = exchange(cross)
    labels = jnp.transpose(cross[:, 4 * tok : 4 * tok + 4, :].astype(jnp.int32), (1, 0, 2))
    far = far_of(labels, cross, tok, rate)
    back = exchange(own(me, labels, cross, far, near, tok, rate))
    near_back = swap(partner(me, labels, near, tok, rate))
    return merge(me, back, near_back, tok)


def local(qkv, routes):
    tok, heads, width = qkv.shape
    head_size = width // 3
    nseq = lax.axis_size("seq")
    clusters = nseq * tok // CLEN
    pairs_dev = heads * tok // CLEN
    chunks = max(1, pairs_dev // clusters)
    split = max(1, clusters // pairs_dev)
    share = tok // split

    def exchange(x):
        return lax.all_to_all(x, "seq", split_axis=0, concat_axis=0, tiled=True)

    labels = jnp.transpose(routes)
    paired = nseq & (nseq - 1) == 0 and nseq * tok // 2 % QB == 0
    if split == 1 and chunks == 2 and paired and tok == 128 and head_size == 128:
        return two_halves(qkv, labels)
    if split == 1:
        rows = exchange(pack(qkv, labels, chunks))
    else:
        group = labels // pairs_dev
        member = group[:, :, None] == jnp.arange(split, dtype=jnp.int32)[None, None, :]
        rank = jnp.cumsum(member.astype(jnp.int32), axis=1) - 1
        slot = group * share + jnp.sum(jnp.where(member, rank, 0), axis=2)
        pick = slot[:, None, :] == jnp.arange(tok, dtype=jnp.int32)[None, :, None]
        moved = jnp.einsum(
            "hst,thd->hsd", pick.astype(jnp.bfloat16), qkv, preferred_element_type=jnp.float32
        ).astype(jnp.bfloat16)
        labels = jnp.sum(jnp.where(pick, labels[:, None, :], 0), axis=2)
        moved = moved.reshape(nseq, share, 3, head_size)
        moved = jnp.transpose(moved, (0, 2, 1, 3)).reshape(nseq, 3 * share, head_size)
        extra = labels.reshape(nseq, 1, share).astype(jnp.bfloat16)
        extra = jnp.pad(extra, ((0, 0), (0, 7), (0, head_size - share)))
        rows = exchange(jnp.concatenate([moved, extra], axis=1))
    first = chunks * 3 * share
    arrived = rows[:, first : first + chunks, :share].astype(jnp.int32)
    arrived = jnp.transpose(arrived, (1, 0, 2)).reshape(chunks, nseq * share // 128, 128)
    back = exchange(attend(arrived, rows, chunks, share)).reshape(heads, tok, head_size)
    if split > 1:
        back = jnp.einsum(
            "hst,hsd->htd", pick.astype(jnp.bfloat16), back, preferred_element_type=jnp.float32
        ).astype(jnp.bfloat16)
    return unpack(back)


def solution(mesh):
    placed = (P(("groups", "seq"), None, None), P(("groups", "seq"), None))
    return jax.shard_map(
        local,
        mesh=mesh,
        in_specs=placed,
        out_specs=P(("groups", "seq"), None, None),
        check_vma=False,
    )
```

```python
import functools
import math

import jax
import jax.numpy as jnp
from jax import lax
from jax.experimental import pallas as pl
from jax.experimental.pallas import tpu as pltpu
from jax.sharding import PartitionSpec as P

CLEN = 1024
QB = 256
STEP = 64
NEG = -1e30


def pack_kernel(x_ref, lab_ref, o_ref, *, chunks):
    tok, heads, width = x_ref.shape
    parts = width // 128
    pad = jnp.zeros((8 - chunks, 128), jnp.float32)
    for dst in range(heads // chunks):
        labels = lab_ref[dst * chunks : (dst + 1) * chunks, :]
        o_ref[dst, pl.ds(chunks * parts * tok, 8), :] = jnp.concatenate(
            [labels.astype(jnp.float32), pad], axis=0
        ).astype(jnp.bfloat16)
    for first in range(0, tok, 32):
        piece = x_ref[first : first + 32].astype(jnp.float32)
        turned = jnp.swapaxes(piece, 0, 1).astype(jnp.bfloat16)
        for head in range(heads):
            for part in range(parts):
                row = (head % chunks * parts + part) * tok + first
                o_ref[head // chunks, row : row + 32, :] = turned[
                    head, :, part * 128 : (part + 1) * 128
                ]


def pack(qkv, labels, chunks):
    tok, heads, width = qkv.shape
    rows = chunks * (width // 128) * tok + 8
    whole = pl.BlockSpec(memory_space=pltpu.VMEM)
    return pl.pallas_call(
        functools.partial(pack_kernel, chunks=chunks),
        out_shape=jax.ShapeDtypeStruct((heads // chunks, rows, 128), jnp.bfloat16),
        in_specs=[whole, whole],
        out_specs=whole,
        compiler_params=pltpu.CompilerParams(vmem_limit_bytes=32 << 20),
        name="pack",
    )(qkv, labels)


def unpack_kernel(x_ref, o_ref):
    o_ref[...] = jnp.swapaxes(x_ref[...].astype(jnp.float32), 0, 1).astype(jnp.bfloat16)


def unpack(back):
    heads, tok, head_size = back.shape
    return pl.pallas_call(
        unpack_kernel,
        out_shape=jax.ShapeDtypeStruct((tok, heads, head_size), jnp.bfloat16),
        grid=(tok // STEP,),
        in_specs=[pl.BlockSpec((heads, STEP, head_size), lambda i: (0, i, 0))],
        out_specs=pl.BlockSpec((STEP, heads, head_size), lambda i: (i, 0, 0)),
        name="unpack",
    )(back)


def attend_kernel(lab_ref, x_ref, o_ref, v_ref, *, share, rate):
    nseq, _, head_size = x_ref.shape
    chunks = lab_ref.shape[0]
    rows = nseq * share
    ramp = lax.broadcasted_iota(jnp.int32, (QB, QB), 1) <= lax.broadcasted_iota(
        jnp.int32, (QB, QB), 0
    )

    def rows_of(chunk, part, first, count):
        base = (chunk * 3 + part) * share
        piece = x_ref[first // share : (first + count) // share, base : base + share, :]
        return piece.reshape(count, head_size)

    for chunk in range(chunks):
        v_ref[chunk, :, :head_size] = rows_of(chunk, 2, 0, rows)
        v_ref[chunk, :, head_size:] = jnp.ones((rows, 128), jnp.bfloat16)

    def score(chunk, block):
        return lax.dot_general(
            rows_of(chunk, 0, block * QB, QB),
            rows_of(chunk, 1, 0, (block + 1) * QB),
            (((1,), (1,)), ((), ())),
            preferred_element_type=jnp.float32,
        )

    def weigh(chunk, block, s):
        row0 = block * QB
        stop = row0 + QB
        lab_q = jnp.concatenate(
            [
                jnp.transpose(jnp.broadcast_to(lab_ref[chunk, i : i + 1, :], (128, 128)))
                for i in range(row0 // 128, stop // 128)
            ],
            axis=0,
        )
        pieces = []
        for i in range(stop // 128):
            keep = lab_q == lab_ref[chunk, i : i + 1, :]
            if i * 128 >= row0:
                keep = keep & ramp[:, i * 128 - row0 : i * 128 - row0 + 128]
            pieces.append(jnp.where(keep, s[:, i * 128 : (i + 1) * 128], NEG))
        peak = functools.reduce(jnp.maximum, pieces)
        peak = jnp.broadcast_to(jnp.max(peak, axis=1, keepdims=True), (QB, 128))
        pieces = [jnp.exp2((piece - peak) * rate).astype(jnp.bfloat16) for piece in pieces]
        return jnp.concatenate(pieces, axis=1)

    def blend(chunk, block, weights):
        row0 = block * QB
        stop = row0 + QB
        both = jnp.dot(weights, v_ref[chunk, :stop, :], preferred_element_type=jnp.float32)
        out = both[:, :head_size] / both[:, head_size:]
        o_ref[row0 // share : stop // share, chunk * share : (chunk + 1) * share] = out.astype(
            jnp.bfloat16
        ).reshape(QB // share, share, head_size)

    blocks = rows // QB
    tasks = [
        (chunk, step if chunk % 2 == 0 else blocks - 1 - step)
        for step in range(blocks)
        for chunk in range(chunks)
    ]
    ahead = score(*tasks[0])
    behind = None
    for place, task in enumerate(tasks):
        s = ahead
        if place + 1 < len(tasks):
            ahead = score(*tasks[place + 1])
        weights = weigh(*task, s)
        if behind is not None:
            blend(*behind)
        behind = (*task, weights)
    blend(*behind)


def attend(labels, x, chunks, share):
    nseq, _, head_size = x.shape
    rows = nseq * share
    rate = math.log2(math.e) / math.sqrt(head_size)
    whole = pl.BlockSpec(memory_space=pltpu.VMEM)
    return pl.pallas_call(
        functools.partial(attend_kernel, share=share, rate=rate),
        out_shape=jax.ShapeDtypeStruct((nseq, chunks * share, head_size), jnp.bfloat16),
        in_specs=[whole, whole],
        out_specs=whole,
        scratch_shapes=[pltpu.VMEM((chunks, rows, head_size + 128), jnp.bfloat16)],
        compiler_params=pltpu.CompilerParams(vmem_limit_bytes=40 << 20),
        name="attend",
    )(labels, x)


def cross_kernel(me_ref, x_ref, lab_ref, o_ref, buf_ref, labs_ref, out_ref, in_sems, out_sems):
    steps, count, heads, _ = buf_ref.shape
    nseq = o_ref.shape[0]
    half = nseq // 2
    tok = steps * count
    lane = pl.multiple_of(jnp.where(me_ref[0] >= half, 0, 128), 128)
    loads = [
        pltpu.make_async_copy(
            x_ref.at[pl.ds(step * count, count), :, pl.ds(lane, 256)],
            buf_ref.at[step],
            in_sems.at[step],
        )
        for step in range(steps)
    ]
    loads.append(pltpu.make_async_copy(lab_ref, labs_ref, in_sems.at[steps]))
    for load in loads:
        load.start()
    stores = []

    def store(row, rows):
        piece = (slice(None), pl.ds(row, rows), slice(None))
        stores.append(
            pltpu.make_async_copy(out_ref.at[piece], o_ref.at[piece], out_sems.at[len(stores)])
        )
        stores[-1].start()

    for step in range(steps):
        loads[step].wait()
        turned = jnp.swapaxes(buf_ref[step].astype(jnp.float32), 0, 1).astype(jnp.bfloat16)
        for part in range(4):
            row = part * tok + step * count
            lanes = slice(part // 2 * 128, part // 2 * 128 + 128)
            for dst in range(nseq):
                out_ref[dst, row : row + count, :] = turned[2 * dst + part % 2, :, lanes]
            store(row, count)
    loads[steps].wait()
    pad = jnp.zeros((4, 128), jnp.float32)
    for dst in range(nseq):
        other = dst ^ half
        labels = [labs_ref[2 * dst : 2 * dst + 2, :], labs_ref[2 * other : 2 * other + 2, :]]
        labels = [piece.astype(jnp.float32) for piece in labels]
        out_ref[dst, 4 * tok : 4 * tok + 8, :] = jnp.concatenate(labels + [pad], axis=0).astype(
            jnp.bfloat16
        )
    store(4 * tok, 8)
    for copy in stores:
        copy.wait()


def near_kernel(me_ref, x_ref, *rest):
    near_refs, turn_ref = rest[:-1], rest[-1]
    tok, heads, width = x_ref.shape
    half = len(near_refs)
    me = me_ref[0]
    for first in range(0, tok, 32):
        piece = x_ref[first : first + 32].astype(jnp.float32)
        turned = jnp.swapaxes(piece, 0, 1).astype(jnp.bfloat16)
        for head in range(heads):
            for part in range(3):
                turn_ref[head, part, first : first + 32, :] = turned[
                    head, :, part * 128 : (part + 1) * 128
                ]
    near_part = jnp.where(me >= half, 2, 0)
    for k, near_ref in enumerate(near_refs):
        dst = me ^ k
        other = dst ^ half
        for j in range(2):
            near_ref[j * tok : (j + 1) * tok, :] = turn_ref[2 * dst + j, near_part]
            for part in range(3):
                row = (2 + 2 * part + j) * tok
                near_ref[row : row + tok, :] = turn_ref[2 * other + j, part]


def spread(me, qkv, labels, nseq):
    tok, heads, width = qkv.shape
    whole = pl.BlockSpec(memory_space=pltpu.VMEM)
    scalar = pl.BlockSpec(memory_space=pltpu.SMEM)
    hbm = pl.BlockSpec(memory_space=pl.ANY)
    params = pltpu.CompilerParams(vmem_limit_bytes=12 << 20)
    cross = pl.pallas_call(
        cross_kernel,
        out_shape=jax.ShapeDtypeStruct((nseq, 4 * tok + 8, 128), jnp.bfloat16),
        in_specs=[scalar, hbm, hbm],
        out_specs=hbm,
        scratch_shapes=[
            pltpu.VMEM((4, tok // 4, heads, 256), jnp.bfloat16),
            pltpu.VMEM(labels.shape, labels.dtype),
            pltpu.VMEM((nseq, 4 * tok + 8, 128), jnp.bfloat16),
            pltpu.SemaphoreType.DMA((5,)),
            pltpu.SemaphoreType.DMA((17,)),
        ],
        compiler_params=pltpu.CompilerParams(vmem_limit_bytes=58 << 20),
        name="cross",
    )(me, qkv, labels)
    near = pl.pallas_call(
        near_kernel,
        out_shape=[jax.ShapeDtypeStruct((8 * tok, 128), jnp.bfloat16)] * (nseq // 2),
        in_specs=[scalar, whole],
        out_specs=[whole] * (nseq // 2),
        scratch_shapes=[pltpu.VMEM((heads, 3, tok, 128), jnp.bfloat16)],
        compiler_params=params,
        name="near",
    )(me, qkv)
    return cross, near


def run_tasks(tasks, score, weigh, blend):
    ahead = score(*tasks[0])
    behind = None
    for place, task in enumerate(tasks):
        s = ahead
        if place + 1 < len(tasks):
            ahead = score(*tasks[place + 1])
        found = weigh(*task, s)
        if behind is not None:
            blend(*behind)
        behind = (*task, *found)
    blend(*behind)


def dot_t(a, b):
    return lax.dot_general(a, b, (((1,), (1,)), ((), ())), preferred_element_type=jnp.float32)


def soften(s, lab_q, lab_k, diagonal, rate):
    pieces = []
    for i, lab in enumerate(lab_k):
        keep = lab_q == lab
        if diagonal is not None and i * 128 >= diagonal:
            lanes = lax.broadcasted_iota(jnp.int32, (QB, 128), 1) + (i * 128 - diagonal)
            keep = keep & (lanes <= lax.broadcasted_iota(jnp.int32, (QB, 128), 0))
        pieces.append(jnp.where(keep, s[:, i * 128 : (i + 1) * 128], NEG))
    peak = functools.reduce(jnp.maximum, pieces)
    peak = jnp.broadcast_to(jnp.max(peak, axis=1, keepdims=True), (QB, 128))
    pieces = [jnp.exp2((piece - peak) * rate).astype(jnp.bfloat16) for piece in pieces]
    return jnp.concatenate(pieces, axis=1), peak


def columns(rows):
    return jnp.concatenate(
        [jnp.transpose(jnp.broadcast_to(row, (128, 128))) for row in rows], axis=0
    )


def three_parts(stats):
    rows = []
    for row in stats:
        for _ in range(3):
            part = row.astype(jnp.bfloat16).astype(jnp.float32)
            rows.append(part)
            row = row - part
    rows.append(jnp.zeros((8 - len(rows), 128), jnp.float32))
    return jnp.concatenate(rows, axis=0).astype(jnp.bfloat16)


def finish(both, peak, rate, tok):
    num, total = both[:, :128], both[:, 128:]
    lse = peak * rate + jnp.log2(total)
    rows = [jnp.transpose(lse[i : i + tok, :])[:1, :] for i in range(0, QB, tok)]
    return num / total, rows


def far_kernel(me_ref, lab_ref, x_ref, o_ref, stat_ref, half_ref, v_ref, *, tok, rate):
    nseq = x_ref.shape[0]
    half = nseq // 2
    span = half * tok
    per = QB // tok
    for j in range(2):
        v_ref[j, :, :128] = x_ref[:half, (2 + j) * tok : (3 + j) * tok, :].reshape(span, 128)
        v_ref[j, :, 128:] = jnp.ones((span, 128), jnp.bfloat16)

    def score(j, block):
        first = half + block * per
        q = x_ref[first : first + per, j * tok : (j + 1) * tok, :].reshape(QB, 128)
        return dot_t(q, x_ref[:half, j * tok : (j + 1) * tok, :].reshape(span, 128))

    def weigh(j, block, s):
        first = half + block * per
        lab_q = columns([lab_ref[j, first + i : first + i + 1, :] for i in range(per)])
        return soften(s, lab_q, [lab_ref[j, i : i + 1, :] for i in range(half)], None, rate)

    def blend(j, block, weights, peak):
        both = jnp.dot(weights, v_ref[j], preferred_element_type=jnp.float32)
        out, rows = finish(both, peak, rate, tok)
        for i, row in enumerate(rows):
            stat_ref[j, block * per + i : block * per + i + 1, :] = row
        o_ref[j, block * QB : (block + 1) * QB, :] = out

    run_tasks([(j, block) for block in range(span // QB) for j in range(2)], score, weigh, blend)
    first = jnp.where(me_ref[0] >= half, half, 0)
    for kind in range(4):
        half_ref[kind] = x_ref[pl.ds(first, half), kind * tok : (kind + 1) * tok, :].reshape(
            span, 128
        )


def far_of(me, labels, x, tok, rate):
    half = x.shape[0] // 2
    whole = pl.BlockSpec(memory_space=pltpu.VMEM)
    return pl.pallas_call(
        functools.partial(far_kernel, tok=tok, rate=rate),
        out_shape=[
            jax.ShapeDtypeStruct((2, half * tok, 128), jnp.float32),
            jax.ShapeDtypeStruct((2, half, 128), jnp.float32),
            jax.ShapeDtypeStruct((4, half * tok, 128), jnp.bfloat16),
        ],
        in_specs=[pl.BlockSpec(memory_space=pltpu.SMEM), whole, whole],
        out_specs=[whole, whole, whole],
        scratch_shapes=[pltpu.VMEM((2, half * tok, 256), jnp.bfloat16)],
        compiler_params=pltpu.CompilerParams(vmem_limit_bytes=16 << 20),
        name="far",
    )(me, labels, x)


def own_kernel(me_ref, lab_ref, far_ref, far_stat_ref, half_ref, *rest, tok, rate):
    half = far_stat_ref.shape[1]
    near_refs, o_ref = rest[:half], rest[half]
    q_ref, v_ref, out_ref, sems = rest[half + 1 :]
    span = half * tok
    per = QB // tok
    me = me_ref[0]
    upper = me >= half
    up = upper.astype(jnp.int32)
    stores = []

    def store(first, count, row, rows):
        piece = (pl.ds(first, count), pl.ds(row, rows), slice(None))
        stores.append(
            pltpu.make_async_copy(out_ref.at[piece], o_ref.at[piece], sems.at[len(stores)])
        )
        stores[-1].start()

    for j in range(2):
        out_ref[pl.ds((1 - up) * half, half), j * tok : (j + 1) * tok, :] = (
            far_ref[j].astype(jnp.bfloat16).reshape(half, tok, 128)
        )
    for i in range(half):
        stats = three_parts([far_stat_ref[j, i : i + 1, :] for j in range(2)])
        out_ref[(1 - up) * half + i, 2 * tok : 2 * tok + 8, :] = stats
        out_ref[up * half + i, 2 * tok : 2 * tok + 8, :] = jnp.zeros((8, 128), jnp.bfloat16)
    store((1 - up) * half, half, 0, 2 * tok + 8)
    store(up * half, half, 2 * tok, 8)
    places = [pl.ds(pl.multiple_of(((me ^ k) % half) * tok, tok), tok) for k in range(half)]

    @pl.when(upper)
    def _():
        for j in range(2):
            q_ref[j] = half_ref[j]
            for place, near_ref in zip(places, near_refs):
                v_ref[j, place, :128] = near_ref[j * tok : (j + 1) * tok, :]

    @pl.when(jnp.logical_not(upper))
    def _():
        for j in range(2):
            v_ref[j, :, :128] = half_ref[2 + j]
            for place, near_ref in zip(places, near_refs):
                q_ref[j, place, :] = near_ref[j * tok : (j + 1) * tok, :]

    for j in range(2):
        v_ref[j, :, 128:] = jnp.ones((span, 128), jnp.bfloat16)

    def lab_of(j, first, count):
        return [lab_ref[j, pl.ds(up * half + first + i, 1), :] for i in range(count)]

    def score(j, block):
        k = half_ref[2 * up + j, : (block + 1) * QB, :]
        return dot_t(q_ref[j, block * QB : (block + 1) * QB, :], k)

    def weigh(j, block, s):
        lab_q = columns(lab_of(j, block * per, per))
        return soften(s, lab_q, lab_of(j, 0, (block + 1) * per), block * QB, rate)

    def blend(j, block, weights, peak):
        both = jnp.dot(
            weights, v_ref[j, : (block + 1) * QB, :], preferred_element_type=jnp.float32
        )
        total = both[:, 128:]
        near = both[:, :128] / total
        rows = [
            far_stat_ref[j, i : i + 1, :] for i in range(block * per, (block + 1) * per)
        ]
        gap = peak * rate + jnp.log2(total) - columns(rows)
        weight = jnp.where(upper, 1.0 / (1.0 + jnp.exp2(gap)), 0.0)
        far = far_ref[j, block * QB : (block + 1) * QB, :]
        out = near + (far - near) * weight
        out_ref[pl.ds(up * half + block * per, per), j * tok : (j + 1) * tok, :] = out.astype(
            jnp.bfloat16
        ).reshape(per, tok, 128)
        store(up * half + block * per, per, j * tok, tok)

    blocks = span // QB
    tasks = [
        (j, block if j == 0 else blocks - 1 - block) for block in range(blocks) for j in range(2)
    ]
    run_tasks(tasks, score, weigh, blend)
    for copy in stores:
        copy.wait()


def own(me, labels, far, near, tok, rate):
    half = len(near)
    nseq = 2 * half
    span = half * tok
    whole = pl.BlockSpec(memory_space=pltpu.VMEM)
    return pl.pallas_call(
        functools.partial(own_kernel, tok=tok, rate=rate),
        out_shape=jax.ShapeDtypeStruct((nseq, 2 * tok + 8, 128), jnp.bfloat16),
        in_specs=[pl.BlockSpec(memory_space=pltpu.SMEM)] + [whole] * (4 + half),
        out_specs=pl.BlockSpec(memory_space=pl.ANY),
        scratch_shapes=[
            pltpu.VMEM((2, span, 128), jnp.bfloat16),
            pltpu.VMEM((2, span, 256), jnp.bfloat16),
            pltpu.VMEM((nseq, 2 * tok + 8, 128), jnp.bfloat16),
            pltpu.SemaphoreType.DMA((2 + 2 * span // QB,)),
        ],
        compiler_params=pltpu.CompilerParams(vmem_limit_bytes=16 << 20),
        name="own",
    )(me, labels, *far, *near)


def partner_kernel(me_ref, lab_ref, *rest, tok, rate):
    half = (len(rest) - 5) // 2
    near_refs, o_refs = rest[:half], rest[half : 2 * half]
    q_ref, k_ref, v_ref, out_ref, stat_ref = rest[2 * half :]
    span = half * tok
    me = me_ref[0]
    up = (me >= half).astype(jnp.int32)
    for j in range(2):
        v_ref[j, :, 128:] = jnp.ones((span, 128), jnp.bfloat16)
        for k, near_ref in enumerate(near_refs):
            place = pl.ds(pl.multiple_of(((me ^ k) % half) * tok, tok), tok)
            q_ref[j, place, :] = near_ref[(2 + j) * tok : (3 + j) * tok, :]
            k_ref[j, place, :] = near_ref[(4 + j) * tok : (5 + j) * tok, :]
            v_ref[j, place, :128] = near_ref[(6 + j) * tok : (7 + j) * tok, :]

    def lab_of(j, first, count):
        return [lab_ref[2 + j, pl.ds(up * half + first + i, 1), :] for i in range(count)]

    per = QB // tok

    def score(j, block):
        return dot_t(q_ref[j, pl.ds(block * QB, QB), :], k_ref[j, : (block + 1) * QB, :])

    def weigh(j, block, s):
        lab_q = columns(lab_of(j, block * per, per))
        return soften(s, lab_q, lab_of(j, 0, (block + 1) * per), block * QB, rate)

    def blend(j, block, weights, peak):
        both = jnp.dot(
            weights, v_ref[j, : (block + 1) * QB, :], preferred_element_type=jnp.float32
        )
        num, total = both[:, :128], both[:, 128:]
        lse = peak * rate + jnp.log2(total)
        out = (num / total).astype(jnp.bfloat16)
        for i in range(per):
            turned = jnp.transpose(lse[i * tok : (i + 1) * tok, :])
            stat_ref[j, block * per + i : block * per + i + 1, :] = turned[:1, :]
            out_ref[block * per + i, j * tok : (j + 1) * tok, :] = out[i * tok : (i + 1) * tok, :]

    blocks = span // QB
    tasks = [
        (j, block if j == 0 else blocks - 1 - block) for block in range(blocks) for j in range(2)
    ]
    run_tasks(tasks, score, weigh, blend)
    for i in range(half):
        stats = three_parts([stat_ref[j, i : i + 1, :] for j in range(2)])
        out_ref[i, 2 * tok : 2 * tok + 8, :] = stats
    for k, o_ref in enumerate(o_refs):
        o_ref[...] = out_ref[(me ^ k) % half]


def partner(me, labels, near, tok, rate):
    half = len(near)
    span = half * tok
    whole = pl.BlockSpec(memory_space=pltpu.VMEM)
    return pl.pallas_call(
        functools.partial(partner_kernel, tok=tok, rate=rate),
        out_shape=[jax.ShapeDtypeStruct((2 * tok + 8, 128), jnp.bfloat16)] * half,
        in_specs=[pl.BlockSpec(memory_space=pltpu.SMEM)] + [whole] * (1 + half),
        out_specs=[whole] * half,
        scratch_shapes=[
            pltpu.VMEM((2, span, 128), jnp.bfloat16),
            pltpu.VMEM((2, span, 128), jnp.bfloat16),
            pltpu.VMEM((2, span, 256), jnp.bfloat16),
            pltpu.VMEM((half, 2 * tok + 8, 128), jnp.bfloat16),
            pltpu.VMEM((2, half, 128), jnp.float32),
        ],
        compiler_params=pltpu.CompilerParams(vmem_limit_bytes=16 << 20),
        name="partner",
    )(me, labels, *near)


def merge_kernel(me_ref, x_ref, *rest, tok):
    nseq = x_ref.shape[0]
    half = nseq // 2
    near_refs, o_ref = rest[:half], rest[half]
    head_ref, out_ref, sems = rest[half + 1 :]
    me = me_ref[0]
    upper = me >= half
    up = upper.astype(jnp.int32)
    down = 1 - up
    heads = 2 * nseq
    for i in range(half):
        for j in range(2):
            head_ref[up * (heads // 2) + 2 * i + j] = x_ref[
                up * half + i, j * tok : (j + 1) * tok, :
            ].astype(jnp.float32)
    for k, near_ref in enumerate(near_refs):
        place = (me ^ k) % half
        far_stats = x_ref[down * half + place, 2 * tok : 2 * tok + 8, :].astype(jnp.float32)
        near_stats = near_ref[2 * tok : 2 * tok + 8, :].astype(jnp.float32)
        for j in range(2):
            near_lse = sum(near_stats[3 * j + c : 3 * j + c + 1, :] for c in range(3))
            far_lse = sum(far_stats[3 * j + c : 3 * j + c + 1, :] for c in range(3))
            weight = jnp.where(upper, 1.0 / (1.0 + jnp.exp2(near_lse - far_lse)), 0.0)
            weight = jnp.transpose(jnp.broadcast_to(weight, (128, tok)))
            far = x_ref[down * half + place, j * tok : (j + 1) * tok, :].astype(jnp.float32)
            near = near_ref[j * tok : (j + 1) * tok, :].astype(jnp.float32)
            head_ref[down * (heads // 2) + 2 * place + j] = near + (far - near) * weight
    stores = []
    for first in range(0, tok, 32):
        piece = head_ref[:, first : first + 32, :]
        out_ref[first : first + 32] = jnp.swapaxes(piece, 0, 1).astype(jnp.bfloat16)
        stores.append(
            pltpu.make_async_copy(
                out_ref.at[pl.ds(first, 32)], o_ref.at[pl.ds(first, 32)], sems.at[len(stores)]
            )
        )
        stores[-1].start()
    for copy in stores:
        copy.wait()


def merge(me, x, near, tok):
    nseq = x.shape[0]
    whole = pl.BlockSpec(memory_space=pltpu.VMEM)
    return pl.pallas_call(
        functools.partial(merge_kernel, tok=tok),
        out_shape=jax.ShapeDtypeStruct((tok, 2 * nseq, 128), jnp.bfloat16),
        in_specs=[pl.BlockSpec(memory_space=pltpu.SMEM)] + [whole] * (1 + nseq // 2),
        out_specs=pl.BlockSpec(memory_space=pl.ANY),
        scratch_shapes=[
            pltpu.VMEM((2 * nseq, tok, 128), jnp.float32),
            pltpu.VMEM((tok, 2 * nseq, 128), jnp.bfloat16),
            pltpu.SemaphoreType.DMA((tok // 32,)),
        ],
        compiler_params=pltpu.CompilerParams(vmem_limit_bytes=12 << 20),
        name="merge",
    )(me, x, *near)


def two_halves(qkv, labels):
    tok, heads, width = qkv.shape
    nseq = lax.axis_size("seq")
    rate = math.log2(math.e) / math.sqrt(width // 3)
    me = lax.axis_index("seq").astype(jnp.int32).reshape(1)

    def exchange(x):
        return lax.all_to_all(x, "seq", split_axis=0, concat_axis=0, tiled=True)

    def swap(blocks):
        moved = list(blocks)
        for k in reversed(range(1, len(blocks))):
            moved[k] = lax.ppermute(blocks[k], "seq", [(i, i ^ k) for i in range(nseq)])
        return moved

    cross, near = spread(me, qkv, labels, nseq)
    near = swap(near)
    cross = exchange(cross)
    labels = jnp.transpose(cross[:, 4 * tok : 4 * tok + 4, :].astype(jnp.int32), (1, 0, 2))
    far = far_of(me, labels, cross, tok, rate)
    back = exchange(own(me, labels, far, near, tok, rate))
    near_back = swap(partner(me, labels, near, tok, rate))
    return merge(me, back, near_back, tok)


def local(qkv, routes):
    tok, heads, width = qkv.shape
    head_size = width // 3
    nseq = lax.axis_size("seq")
    clusters = nseq * tok // CLEN
    pairs_dev = heads * tok // CLEN
    chunks = max(1, pairs_dev // clusters)
    split = max(1, clusters // pairs_dev)
    share = tok // split

    def exchange(x):
        return lax.all_to_all(x, "seq", split_axis=0, concat_axis=0, tiled=True)

    labels = jnp.transpose(routes)
    paired = nseq & (nseq - 1) == 0 and nseq * tok // 2 % QB == 0
    if split == 1 and chunks == 2 and paired and tok == 128 and head_size == 128:
        return two_halves(qkv, labels)
    if split == 1:
        rows = exchange(pack(qkv, labels, chunks))
    else:
        group = labels // pairs_dev
        member = group[:, :, None] == jnp.arange(split, dtype=jnp.int32)[None, None, :]
        rank = jnp.cumsum(member.astype(jnp.int32), axis=1) - 1
        slot = group * share + jnp.sum(jnp.where(member, rank, 0), axis=2)
        pick = slot[:, None, :] == jnp.arange(tok, dtype=jnp.int32)[None, :, None]
        moved = jnp.einsum(
            "hst,thd->hsd", pick.astype(jnp.bfloat16), qkv, preferred_element_type=jnp.float32
        ).astype(jnp.bfloat16)
        labels = jnp.sum(jnp.where(pick, labels[:, None, :], 0), axis=2)
        moved = moved.reshape(nseq, share, 3, head_size)
        moved = jnp.transpose(moved, (0, 2, 1, 3)).reshape(nseq, 3 * share, head_size)
        extra = labels.reshape(nseq, 1, share).astype(jnp.bfloat16)
        extra = jnp.pad(extra, ((0, 0), (0, 7), (0, head_size - share)))
        rows = exchange(jnp.concatenate([moved, extra], axis=1))
    first = chunks * 3 * share
    arrived = rows[:, first : first + chunks, :share].astype(jnp.int32)
    arrived = jnp.transpose(arrived, (1, 0, 2)).reshape(chunks, nseq * share // 128, 128)
    back = exchange(attend(arrived, rows, chunks, share)).reshape(heads, tok, head_size)
    if split > 1:
        back = jnp.einsum(
            "hst,hsd->htd", pick.astype(jnp.bfloat16), back, preferred_element_type=jnp.float32
        ).astype(jnp.bfloat16)
    return unpack(back)


def solution(mesh):
    placed = (P(("groups", "seq"), None, None), P(("groups", "seq"), None))
    return jax.shard_map(
        local,
        mesh=mesh,
        in_specs=placed,
        out_specs=P(("groups", "seq"), None, None),
        check_vma=False,
    )
```

```python
import functools
import math

import jax
import jax.numpy as jnp
from jax import lax
from jax.experimental import pallas as pl
from jax.experimental.pallas import tpu as pltpu
from jax.sharding import PartitionSpec as P

CLEN = 1024
QB = 256
STEP = 64
HOPS = (0, 2, 3, 6, 7, 4, 5, 1)
NEG = -1e30


def pack_kernel(x_ref, lab_ref, o_ref, *, chunks):
    tok, heads, width = x_ref.shape
    parts = width // 128
    pad = jnp.zeros((8 - chunks, 128), jnp.float32)
    for dst in range(heads // chunks):
        labels = lab_ref[dst * chunks : (dst + 1) * chunks, :]
        o_ref[dst, pl.ds(chunks * parts * tok, 8), :] = jnp.concatenate(
            [labels.astype(jnp.float32), pad], axis=0
        ).astype(jnp.bfloat16)
    for first in range(0, tok, 32):
        piece = x_ref[first : first + 32].astype(jnp.float32)
        turned = jnp.swapaxes(piece, 0, 1).astype(jnp.bfloat16)
        for head in range(heads):
            for part in range(parts):
                row = (head % chunks * parts + part) * tok + first
                o_ref[head // chunks, row : row + 32, :] = turned[
                    head, :, part * 128 : (part + 1) * 128
                ]


def pack(qkv, labels, chunks):
    tok, heads, width = qkv.shape
    rows = chunks * (width // 128) * tok + 8
    whole = pl.BlockSpec(memory_space=pltpu.VMEM)
    return pl.pallas_call(
        functools.partial(pack_kernel, chunks=chunks),
        out_shape=jax.ShapeDtypeStruct((heads // chunks, rows, 128), jnp.bfloat16),
        in_specs=[whole, whole],
        out_specs=whole,
        compiler_params=pltpu.CompilerParams(vmem_limit_bytes=32 << 20),
        name="pack",
    )(qkv, labels)


def unpack_kernel(x_ref, o_ref):
    o_ref[...] = jnp.swapaxes(x_ref[...].astype(jnp.float32), 0, 1).astype(jnp.bfloat16)


def unpack(back):
    heads, tok, head_size = back.shape
    return pl.pallas_call(
        unpack_kernel,
        out_shape=jax.ShapeDtypeStruct((tok, heads, head_size), jnp.bfloat16),
        grid=(tok // STEP,),
        in_specs=[pl.BlockSpec((heads, STEP, head_size), lambda i: (0, i, 0))],
        out_specs=pl.BlockSpec((STEP, heads, head_size), lambda i: (i, 0, 0)),
        name="unpack",
    )(back)


def attend_kernel(lab_ref, x_ref, o_ref, v_ref, *, share, rate):
    nseq, _, head_size = x_ref.shape
    chunks = lab_ref.shape[0]
    rows = nseq * share
    ramp = lax.broadcasted_iota(jnp.int32, (QB, QB), 1) <= lax.broadcasted_iota(
        jnp.int32, (QB, QB), 0
    )

    def rows_of(chunk, part, first, count):
        base = (chunk * 3 + part) * share
        piece = x_ref[first // share : (first + count) // share, base : base + share, :]
        return piece.reshape(count, head_size)

    for chunk in range(chunks):
        v_ref[chunk, :, :head_size] = rows_of(chunk, 2, 0, rows)
        v_ref[chunk, :, head_size:] = jnp.ones((rows, 128), jnp.bfloat16)

    def score(chunk, block):
        return lax.dot_general(
            rows_of(chunk, 0, block * QB, QB),
            rows_of(chunk, 1, 0, (block + 1) * QB),
            (((1,), (1,)), ((), ())),
            preferred_element_type=jnp.float32,
        )

    def weigh(chunk, block, s):
        row0 = block * QB
        stop = row0 + QB
        lab_q = jnp.concatenate(
            [
                jnp.transpose(jnp.broadcast_to(lab_ref[chunk, i : i + 1, :], (128, 128)))
                for i in range(row0 // 128, stop // 128)
            ],
            axis=0,
        )
        pieces = []
        for i in range(stop // 128):
            keep = lab_q == lab_ref[chunk, i : i + 1, :]
            if i * 128 >= row0:
                keep = keep & ramp[:, i * 128 - row0 : i * 128 - row0 + 128]
            pieces.append(jnp.where(keep, s[:, i * 128 : (i + 1) * 128], NEG))
        peak = functools.reduce(jnp.maximum, pieces)
        peak = jnp.broadcast_to(jnp.max(peak, axis=1, keepdims=True), (QB, 128))
        pieces = [jnp.exp2((piece - peak) * rate).astype(jnp.bfloat16) for piece in pieces]
        return jnp.concatenate(pieces, axis=1)

    def blend(chunk, block, weights):
        row0 = block * QB
        stop = row0 + QB
        both = jnp.dot(weights, v_ref[chunk, :stop, :], preferred_element_type=jnp.float32)
        out = both[:, :head_size] / both[:, head_size:]
        o_ref[row0 // share : stop // share, chunk * share : (chunk + 1) * share] = out.astype(
            jnp.bfloat16
        ).reshape(QB // share, share, head_size)

    blocks = rows // QB
    tasks = [
        (chunk, step if chunk % 2 == 0 else blocks - 1 - step)
        for step in range(blocks)
        for chunk in range(chunks)
    ]
    ahead = score(*tasks[0])
    behind = None
    for place, task in enumerate(tasks):
        s = ahead
        if place + 1 < len(tasks):
            ahead = score(*tasks[place + 1])
        weights = weigh(*task, s)
        if behind is not None:
            blend(*behind)
        behind = (*task, weights)
    blend(*behind)


def attend(labels, x, chunks, share):
    nseq, _, head_size = x.shape
    rows = nseq * share
    rate = math.log2(math.e) / math.sqrt(head_size)
    whole = pl.BlockSpec(memory_space=pltpu.VMEM)
    return pl.pallas_call(
        functools.partial(attend_kernel, share=share, rate=rate),
        out_shape=jax.ShapeDtypeStruct((nseq, chunks * share, head_size), jnp.bfloat16),
        in_specs=[whole, whole],
        out_specs=whole,
        scratch_shapes=[pltpu.VMEM((chunks, rows, head_size + 128), jnp.bfloat16)],
        compiler_params=pltpu.CompilerParams(vmem_limit_bytes=40 << 20),
        name="attend",
    )(labels, x)


def cross_kernel(me_ref, x_ref, lab_ref, o_ref, buf_ref, labs_ref, out_ref, in_sems, out_sems):
    steps, count, heads, _ = buf_ref.shape
    nseq = o_ref.shape[0]
    half = nseq // 2
    tok = steps * count
    lane = pl.multiple_of(jnp.where(me_ref[0] >= half, 0, 128), 128)
    loads = [
        pltpu.make_async_copy(
            x_ref.at[pl.ds(step * count, count), :, pl.ds(lane, 256)],
            buf_ref.at[step],
            in_sems.at[step],
        )
        for step in range(steps)
    ]
    loads.append(pltpu.make_async_copy(lab_ref, labs_ref, in_sems.at[steps]))
    for load in loads:
        load.start()
    stores = []

    def store(row, rows):
        piece = (slice(None), pl.ds(row, rows), slice(None))
        stores.append(
            pltpu.make_async_copy(out_ref.at[piece], o_ref.at[piece], out_sems.at[len(stores)])
        )
        stores[-1].start()

    for step in range(steps):
        loads[step].wait()
        turned = jnp.swapaxes(buf_ref[step].astype(jnp.float32), 0, 1).astype(jnp.bfloat16)
        for part in range(4):
            row = part * tok + step * count
            lanes = slice(part // 2 * 128, part // 2 * 128 + 128)
            for dst in range(nseq):
                out_ref[dst, row : row + count, :] = turned[2 * dst + part % 2, :, lanes]
            store(row, count)
    loads[steps].wait()
    pad = jnp.zeros((4, 128), jnp.float32)
    for dst in range(nseq):
        other = dst ^ half
        labels = [labs_ref[2 * dst : 2 * dst + 2, :], labs_ref[2 * other : 2 * other + 2, :]]
        labels = [piece.astype(jnp.float32) for piece in labels]
        out_ref[dst, 4 * tok : 4 * tok + 8, :] = jnp.concatenate(labels + [pad], axis=0).astype(
            jnp.bfloat16
        )
    store(4 * tok, 8)
    for copy in stores:
        copy.wait()


def near_kernel(me_ref, x_ref, *rest):
    near_refs, turn_ref = rest[:-1], rest[-1]
    tok, heads, width = x_ref.shape
    half = len(near_refs)
    me = me_ref[0]
    for first in range(0, tok, 32):
        piece = x_ref[first : first + 32].astype(jnp.float32)
        turned = jnp.swapaxes(piece, 0, 1).astype(jnp.bfloat16)
        for head in range(heads):
            for part in range(3):
                turn_ref[head, part, first : first + 32, :] = turned[
                    head, :, part * 128 : (part + 1) * 128
                ]
    near_part = jnp.where(me >= half, 2, 0)
    for k, near_ref in enumerate(near_refs):
        dst = me ^ k
        other = dst ^ half
        for j in range(2):
            near_ref[j * tok : (j + 1) * tok, :] = turn_ref[2 * dst + j, near_part]
            for part in range(3):
                row = (2 + 2 * part + j) * tok
                near_ref[row : row + tok, :] = turn_ref[2 * other + j, part]


def spread(me, qkv, labels, nseq):
    tok, heads, width = qkv.shape
    whole = pl.BlockSpec(memory_space=pltpu.VMEM)
    scalar = pl.BlockSpec(memory_space=pltpu.SMEM)
    hbm = pl.BlockSpec(memory_space=pl.ANY)
    params = pltpu.CompilerParams(vmem_limit_bytes=12 << 20)
    cross = pl.pallas_call(
        cross_kernel,
        out_shape=jax.ShapeDtypeStruct((nseq, 4 * tok + 8, 128), jnp.bfloat16),
        in_specs=[scalar, hbm, hbm],
        out_specs=hbm,
        scratch_shapes=[
            pltpu.VMEM((4, tok // 4, heads, 256), jnp.bfloat16),
            pltpu.VMEM(labels.shape, labels.dtype),
            pltpu.VMEM((nseq, 4 * tok + 8, 128), jnp.bfloat16),
            pltpu.SemaphoreType.DMA((5,)),
            pltpu.SemaphoreType.DMA((17,)),
        ],
        compiler_params=pltpu.CompilerParams(vmem_limit_bytes=58 << 20),
        name="cross",
    )(me, qkv, labels)
    near = pl.pallas_call(
        near_kernel,
        out_shape=[jax.ShapeDtypeStruct((8 * tok, 128), jnp.bfloat16)] * (nseq // 2),
        in_specs=[scalar, whole],
        out_specs=[whole] * (nseq // 2),
        scratch_shapes=[pltpu.VMEM((heads, 3, tok, 128), jnp.bfloat16)],
        compiler_params=params,
        name="near",
    )(me, qkv)
    return cross, near


def run_tasks(tasks, score, weigh, blend):
    ahead = score(*tasks[0])
    behind = None
    for place, task in enumerate(tasks):
        s = ahead
        if place + 1 < len(tasks):
            ahead = score(*tasks[place + 1])
        found = weigh(*task, s)
        if behind is not None:
            blend(*behind)
        behind = (*task, *found)
    blend(*behind)


def dot_t(a, b):
    return lax.dot_general(a, b, (((1,), (1,)), ((), ())), preferred_element_type=jnp.float32)


def soften(s, lab_q, lab_k, diagonal, rate):
    pieces = []
    for i, lab in enumerate(lab_k):
        keep = lab_q == lab
        if diagonal is not None and i * 128 >= diagonal:
            lanes = lax.broadcasted_iota(jnp.int32, (QB, 128), 1) + (i * 128 - diagonal)
            keep = keep & (lanes <= lax.broadcasted_iota(jnp.int32, (QB, 128), 0))
        pieces.append(jnp.where(keep, s[:, i * 128 : (i + 1) * 128], NEG))
    peak = functools.reduce(jnp.maximum, pieces)
    peak = jnp.broadcast_to(jnp.max(peak, axis=1, keepdims=True), (QB, 128))
    pieces = [jnp.exp2((piece - peak) * rate).astype(jnp.bfloat16) for piece in pieces]
    return jnp.concatenate(pieces, axis=1), peak


def columns(rows):
    return jnp.concatenate(
        [jnp.transpose(jnp.broadcast_to(row, (128, 128))) for row in rows], axis=0
    )


def three_parts(stats):
    rows = []
    for row in stats:
        for _ in range(3):
            part = row.astype(jnp.bfloat16).astype(jnp.float32)
            rows.append(part)
            row = row - part
    rows.append(jnp.zeros((8 - len(rows), 128), jnp.float32))
    return jnp.concatenate(rows, axis=0).astype(jnp.bfloat16)


def finish(both, peak, rate, tok):
    num, total = both[:, :128], both[:, 128:]
    lse = peak * rate + jnp.log2(total)
    rows = [jnp.transpose(lse[i : i + tok, :])[:1, :] for i in range(0, QB, tok)]
    return num / total, rows


def far_kernel(me_ref, lab_ref, x_ref, o_ref, stat_ref, half_ref, v_ref, *, tok, rate):
    nseq = x_ref.shape[0]
    half = nseq // 2
    span = half * tok
    per = QB // tok
    for j in range(2):
        v_ref[j, :, :128] = x_ref[:half, (2 + j) * tok : (3 + j) * tok, :].reshape(span, 128)
        v_ref[j, :, 128:] = jnp.ones((span, 128), jnp.bfloat16)

    def score(j, block):
        first = half + block * per
        q = x_ref[first : first + per, j * tok : (j + 1) * tok, :].reshape(QB, 128)
        return dot_t(q, x_ref[:half, j * tok : (j + 1) * tok, :].reshape(span, 128))

    def weigh(j, block, s):
        first = half + block * per
        lab_q = columns([lab_ref[j, first + i : first + i + 1, :] for i in range(per)])
        return soften(s, lab_q, [lab_ref[j, i : i + 1, :] for i in range(half)], None, rate)

    def blend(j, block, weights, peak):
        both = jnp.dot(weights, v_ref[j], preferred_element_type=jnp.float32)
        out, rows = finish(both, peak, rate, tok)
        for i, row in enumerate(rows):
            stat_ref[j, block * per + i : block * per + i + 1, :] = row
        o_ref[j, block * QB : (block + 1) * QB, :] = out

    run_tasks([(j, block) for block in range(span // QB) for j in range(2)], score, weigh, blend)
    first = jnp.where(me_ref[0] >= half, half, 0)
    for kind in range(4):
        half_ref[kind] = x_ref[pl.ds(first, half), kind * tok : (kind + 1) * tok, :].reshape(
            span, 128
        )


def far_of(me, labels, x, tok, rate):
    half = x.shape[0] // 2
    whole = pl.BlockSpec(memory_space=pltpu.VMEM)
    return pl.pallas_call(
        functools.partial(far_kernel, tok=tok, rate=rate),
        out_shape=[
            jax.ShapeDtypeStruct((2, half * tok, 128), jnp.float32),
            jax.ShapeDtypeStruct((2, half, 128), jnp.float32),
            jax.ShapeDtypeStruct((4, half * tok, 128), jnp.bfloat16),
        ],
        in_specs=[pl.BlockSpec(memory_space=pltpu.SMEM), whole, whole],
        out_specs=[whole, whole, whole],
        scratch_shapes=[pltpu.VMEM((2, half * tok, 256), jnp.bfloat16)],
        compiler_params=pltpu.CompilerParams(vmem_limit_bytes=16 << 20),
        name="far",
    )(me, labels, x)


def own_kernel(me_ref, lab_ref, far_ref, far_stat_ref, half_ref, *rest, tok, rate):
    half = far_stat_ref.shape[1]
    near_refs, o_ref = rest[:half], rest[half]
    q_ref, v_ref, out_ref, sems = rest[half + 1 :]
    span = half * tok
    per = QB // tok
    me = me_ref[0]
    upper = me >= half
    up = upper.astype(jnp.int32)
    stores = []

    def store(first, count, row, rows):
        piece = (pl.ds(first, count), pl.ds(row, rows), slice(None))
        stores.append(
            pltpu.make_async_copy(out_ref.at[piece], o_ref.at[piece], sems.at[len(stores)])
        )
        stores[-1].start()

    for j in range(2):
        out_ref[pl.ds((1 - up) * half, half), j * tok : (j + 1) * tok, :] = (
            far_ref[j].astype(jnp.bfloat16).reshape(half, tok, 128)
        )
    for i in range(half):
        stats = three_parts([far_stat_ref[j, i : i + 1, :] for j in range(2)])
        out_ref[(1 - up) * half + i, 2 * tok : 2 * tok + 8, :] = stats
        out_ref[up * half + i, 2 * tok : 2 * tok + 8, :] = jnp.zeros((8, 128), jnp.bfloat16)
    store((1 - up) * half, half, 0, 2 * tok + 8)
    store(up * half, half, 2 * tok, 8)
    places = [pl.ds(pl.multiple_of(((me ^ k) % half) * tok, tok), tok) for k in range(half)]

    @pl.when(upper)
    def _():
        for j in range(2):
            q_ref[j] = half_ref[j]
            for place, near_ref in zip(places, near_refs):
                v_ref[j, place, :128] = near_ref[j * tok : (j + 1) * tok, :]

    @pl.when(jnp.logical_not(upper))
    def _():
        for j in range(2):
            v_ref[j, :, :128] = half_ref[2 + j]
            for place, near_ref in zip(places, near_refs):
                q_ref[j, place, :] = near_ref[j * tok : (j + 1) * tok, :]

    for j in range(2):
        v_ref[j, :, 128:] = jnp.ones((span, 128), jnp.bfloat16)

    def lab_of(j, first, count):
        return [lab_ref[j, pl.ds(up * half + first + i, 1), :] for i in range(count)]

    def score(j, block):
        k = half_ref[2 * up + j, : (block + 1) * QB, :]
        return dot_t(q_ref[j, block * QB : (block + 1) * QB, :], k)

    def weigh(j, block, s):
        lab_q = columns(lab_of(j, block * per, per))
        return soften(s, lab_q, lab_of(j, 0, (block + 1) * per), block * QB, rate)

    def blend(j, block, weights, peak):
        both = jnp.dot(
            weights, v_ref[j, : (block + 1) * QB, :], preferred_element_type=jnp.float32
        )
        total = both[:, 128:]
        near = both[:, :128] / total
        rows = [
            far_stat_ref[j, i : i + 1, :] for i in range(block * per, (block + 1) * per)
        ]
        gap = peak * rate + jnp.log2(total) - columns(rows)
        weight = jnp.where(upper, 1.0 / (1.0 + jnp.exp2(gap)), 0.0)
        far = far_ref[j, block * QB : (block + 1) * QB, :]
        out = near + (far - near) * weight
        out_ref[pl.ds(up * half + block * per, per), j * tok : (j + 1) * tok, :] = out.astype(
            jnp.bfloat16
        ).reshape(per, tok, 128)
        store(up * half + block * per, per, j * tok, tok)

    blocks = span // QB
    tasks = [
        (j, block if j == 0 else blocks - 1 - block) for block in range(blocks) for j in range(2)
    ]
    run_tasks(tasks, score, weigh, blend)
    for copy in stores:
        copy.wait()


def own(me, labels, far, near, tok, rate):
    half = len(near)
    nseq = 2 * half
    span = half * tok
    whole = pl.BlockSpec(memory_space=pltpu.VMEM)
    return pl.pallas_call(
        functools.partial(own_kernel, tok=tok, rate=rate),
        out_shape=jax.ShapeDtypeStruct((nseq, 2 * tok + 8, 128), jnp.bfloat16),
        in_specs=[pl.BlockSpec(memory_space=pltpu.SMEM)] + [whole] * (4 + half),
        out_specs=pl.BlockSpec(memory_space=pl.ANY),
        scratch_shapes=[
            pltpu.VMEM((2, span, 128), jnp.bfloat16),
            pltpu.VMEM((2, span, 256), jnp.bfloat16),
            pltpu.VMEM((nseq, 2 * tok + 8, 128), jnp.bfloat16),
            pltpu.SemaphoreType.DMA((2 + 2 * span // QB,)),
        ],
        compiler_params=pltpu.CompilerParams(vmem_limit_bytes=16 << 20),
        name="own",
    )(me, labels, *far, *near)


def partner_kernel(me_ref, lab_ref, *rest, tok, rate):
    half = (len(rest) - 5) // 2
    near_refs, o_refs = rest[:half], rest[half : 2 * half]
    q_ref, k_ref, v_ref, out_ref, stat_ref = rest[2 * half :]
    span = half * tok
    me = me_ref[0]
    up = (me >= half).astype(jnp.int32)
    for j in range(2):
        v_ref[j, :, 128:] = jnp.ones((span, 128), jnp.bfloat16)
        for k, near_ref in enumerate(near_refs):
            place = pl.ds(pl.multiple_of(((me ^ k) % half) * tok, tok), tok)
            q_ref[j, place, :] = near_ref[(2 + j) * tok : (3 + j) * tok, :]
            k_ref[j, place, :] = near_ref[(4 + j) * tok : (5 + j) * tok, :]
            v_ref[j, place, :128] = near_ref[(6 + j) * tok : (7 + j) * tok, :]

    def lab_of(j, first, count):
        return [lab_ref[2 + j, pl.ds(up * half + first + i, 1), :] for i in range(count)]

    per = QB // tok

    def score(j, block):
        return dot_t(q_ref[j, pl.ds(block * QB, QB), :], k_ref[j, : (block + 1) * QB, :])

    def weigh(j, block, s):
        lab_q = columns(lab_of(j, block * per, per))
        return soften(s, lab_q, lab_of(j, 0, (block + 1) * per), block * QB, rate)

    def blend(j, block, weights, peak):
        both = jnp.dot(
            weights, v_ref[j, : (block + 1) * QB, :], preferred_element_type=jnp.float32
        )
        num, total = both[:, :128], both[:, 128:]
        lse = peak * rate + jnp.log2(total)
        out = (num / total).astype(jnp.bfloat16)
        for i in range(per):
            turned = jnp.transpose(lse[i * tok : (i + 1) * tok, :])
            stat_ref[j, block * per + i : block * per + i + 1, :] = turned[:1, :]
            out_ref[block * per + i, j * tok : (j + 1) * tok, :] = out[i * tok : (i + 1) * tok, :]

    blocks = span // QB
    tasks = [
        (j, block if j == 0 else blocks - 1 - block) for block in range(blocks) for j in range(2)
    ]
    run_tasks(tasks, score, weigh, blend)
    for i in range(half):
        stats = three_parts([stat_ref[j, i : i + 1, :] for j in range(2)])
        out_ref[i, 2 * tok : 2 * tok + 8, :] = stats
    for k, o_ref in enumerate(o_refs):
        o_ref[...] = out_ref[(me ^ k) % half]


def partner(me, labels, near, tok, rate):
    half = len(near)
    span = half * tok
    whole = pl.BlockSpec(memory_space=pltpu.VMEM)
    return pl.pallas_call(
        functools.partial(partner_kernel, tok=tok, rate=rate),
        out_shape=[jax.ShapeDtypeStruct((2 * tok + 8, 128), jnp.bfloat16)] * half,
        in_specs=[pl.BlockSpec(memory_space=pltpu.SMEM)] + [whole] * (1 + half),
        out_specs=[whole] * half,
        scratch_shapes=[
            pltpu.VMEM((2, span, 128), jnp.bfloat16),
            pltpu.VMEM((2, span, 128), jnp.bfloat16),
            pltpu.VMEM((2, span, 256), jnp.bfloat16),
            pltpu.VMEM((half, 2 * tok + 8, 128), jnp.bfloat16),
            pltpu.VMEM((2, half, 128), jnp.float32),
        ],
        compiler_params=pltpu.CompilerParams(vmem_limit_bytes=16 << 20),
        name="partner",
    )(me, labels, *near)


def merge_kernel(me_ref, x_ref, *rest, tok):
    nseq = x_ref.shape[0]
    half = nseq // 2
    near_refs, o_ref = rest[:half], rest[half]
    head_ref, out_ref, sems = rest[half + 1 :]
    me = me_ref[0]
    upper = me >= half
    up = upper.astype(jnp.int32)
    down = 1 - up
    heads = 2 * nseq
    for i in range(half):
        for j in range(2):
            head_ref[up * (heads // 2) + 2 * i + j] = x_ref[
                up * half + i, j * tok : (j + 1) * tok, :
            ].astype(jnp.float32)
    for k, near_ref in zip(HOPS, near_refs):
        place = (me ^ k) % half
        far_stats = x_ref[down * half + place, 2 * tok : 2 * tok + 8, :].astype(jnp.float32)
        near_stats = near_ref[2 * tok : 2 * tok + 8, :].astype(jnp.float32)
        for j in range(2):
            near_lse = sum(near_stats[3 * j + c : 3 * j + c + 1, :] for c in range(3))
            far_lse = sum(far_stats[3 * j + c : 3 * j + c + 1, :] for c in range(3))
            weight = jnp.where(upper, 1.0 / (1.0 + jnp.exp2(near_lse - far_lse)), 0.0)
            weight = jnp.transpose(jnp.broadcast_to(weight, (128, tok)))
            far = x_ref[down * half + place, j * tok : (j + 1) * tok, :].astype(jnp.float32)
            near = near_ref[j * tok : (j + 1) * tok, :].astype(jnp.float32)
            head_ref[down * (heads // 2) + 2 * place + j] = near + (far - near) * weight
    stores = []
    for first in range(0, tok, 32):
        piece = head_ref[:, first : first + 32, :]
        out_ref[first : first + 32] = jnp.swapaxes(piece, 0, 1).astype(jnp.bfloat16)
        stores.append(
            pltpu.make_async_copy(
                out_ref.at[pl.ds(first, 32)], o_ref.at[pl.ds(first, 32)], sems.at[len(stores)]
            )
        )
        stores[-1].start()
    for copy in stores:
        copy.wait()


def merge(me, x, near, tok):
    nseq = x.shape[0]
    whole = pl.BlockSpec(memory_space=pltpu.VMEM)
    return pl.pallas_call(
        functools.partial(merge_kernel, tok=tok),
        out_shape=jax.ShapeDtypeStruct((tok, 2 * nseq, 128), jnp.bfloat16),
        in_specs=[pl.BlockSpec(memory_space=pltpu.SMEM)] + [whole] * (1 + nseq // 2),
        out_specs=pl.BlockSpec(memory_space=pl.ANY),
        scratch_shapes=[
            pltpu.VMEM((2 * nseq, tok, 128), jnp.float32),
            pltpu.VMEM((tok, 2 * nseq, 128), jnp.bfloat16),
            pltpu.SemaphoreType.DMA((tok // 32,)),
        ],
        compiler_params=pltpu.CompilerParams(vmem_limit_bytes=12 << 20),
        name="merge",
    )(me, x, *near)


def two_halves(qkv, labels):
    tok, heads, width = qkv.shape
    nseq = lax.axis_size("seq")
    rate = math.log2(math.e) / math.sqrt(width // 3)
    me = lax.axis_index("seq").astype(jnp.int32).reshape(1)

    def exchange(x):
        return lax.all_to_all(x, "seq", split_axis=0, concat_axis=0, tiled=True)

    def swap(blocks):
        moved = list(blocks)
        for k in reversed(range(1, len(blocks))):
            moved[k] = lax.ppermute(blocks[k], "seq", [(i, i ^ k) for i in range(nseq)])
        return moved

    cross, near = spread(me, qkv, labels, nseq)
    near = swap(near)
    cross = exchange(cross)
    labels = jnp.transpose(cross[:, 4 * tok : 4 * tok + 4, :].astype(jnp.int32), (1, 0, 2))
    far = far_of(me, labels, cross, tok, rate)
    back = exchange(own(me, labels, far, near, tok, rate))
    near_back = swap(partner(me, labels, near, tok, rate))
    return merge(me, back, [near_back[k] for k in HOPS], tok)


def local(qkv, routes):
    tok, heads, width = qkv.shape
    head_size = width // 3
    nseq = lax.axis_size("seq")
    clusters = nseq * tok // CLEN
    pairs_dev = heads * tok // CLEN
    chunks = max(1, pairs_dev // clusters)
    split = max(1, clusters // pairs_dev)
    share = tok // split

    def exchange(x):
        return lax.all_to_all(x, "seq", split_axis=0, concat_axis=0, tiled=True)

    labels = jnp.transpose(routes)
    paired = nseq == 2 * len(HOPS) and nseq * tok // 2 % QB == 0
    if split == 1 and chunks == 2 and paired and tok == 128 and head_size == 128:
        return two_halves(qkv, labels)
    if split == 1:
        rows = exchange(pack(qkv, labels, chunks))
    else:
        group = labels // pairs_dev
        member = group[:, :, None] == jnp.arange(split, dtype=jnp.int32)[None, None, :]
        rank = jnp.cumsum(member.astype(jnp.int32), axis=1) - 1
        slot = group * share + jnp.sum(jnp.where(member, rank, 0), axis=2)
        pick = slot[:, None, :] == jnp.arange(tok, dtype=jnp.int32)[None, :, None]
        moved = jnp.einsum(
            "hst,thd->hsd", pick.astype(jnp.bfloat16), qkv, preferred_element_type=jnp.float32
        ).astype(jnp.bfloat16)
        labels = jnp.sum(jnp.where(pick, labels[:, None, :], 0), axis=2)
        moved = moved.reshape(nseq, share, 3, head_size)
        moved = jnp.transpose(moved, (0, 2, 1, 3)).reshape(nseq, 3 * share, head_size)
        extra = labels.reshape(nseq, 1, share).astype(jnp.bfloat16)
        extra = jnp.pad(extra, ((0, 0), (0, 7), (0, head_size - share)))
        rows = exchange(jnp.concatenate([moved, extra], axis=1))
    first = chunks * 3 * share
    arrived = rows[:, first : first + chunks, :share].astype(jnp.int32)
    arrived = jnp.transpose(arrived, (1, 0, 2)).reshape(chunks, nseq * share // 128, 128)
    back = exchange(attend(arrived, rows, chunks, share)).reshape(heads, tok, head_size)
    if split > 1:
        back = jnp.einsum(
            "hst,hsd->htd", pick.astype(jnp.bfloat16), back, preferred_element_type=jnp.float32
        ).astype(jnp.bfloat16)
    return unpack(back)


def solution(mesh):
    placed = (P(("groups", "seq"), None, None), P(("groups", "seq"), None))
    return jax.shard_map(
        local,
        mesh=mesh,
        in_specs=placed,
        out_specs=P(("groups", "seq"), None, None),
        check_vma=False,
    )
```

```python
import functools
import math

import jax
import jax.numpy as jnp
from jax import lax
from jax.experimental import pallas as pl
from jax.experimental.pallas import tpu as pltpu
from jax.sharding import PartitionSpec as P

CLEN = 1024
QB = 256
STEP = 64
HOPS = (0, 2, 6, 3, 7, 4, 5, 1)
NEG = -1e30


def pack_kernel(x_ref, lab_ref, o_ref, *, chunks):
    tok, heads, width = x_ref.shape
    parts = width // 128
    pad = jnp.zeros((8 - chunks, 128), jnp.float32)
    for dst in range(heads // chunks):
        labels = lab_ref[dst * chunks : (dst + 1) * chunks, :]
        o_ref[dst, pl.ds(chunks * parts * tok, 8), :] = jnp.concatenate(
            [labels.astype(jnp.float32), pad], axis=0
        ).astype(jnp.bfloat16)
    for first in range(0, tok, 32):
        piece = x_ref[first : first + 32].astype(jnp.float32)
        turned = jnp.swapaxes(piece, 0, 1).astype(jnp.bfloat16)
        for head in range(heads):
            for part in range(parts):
                row = (head % chunks * parts + part) * tok + first
                o_ref[head // chunks, row : row + 32, :] = turned[
                    head, :, part * 128 : (part + 1) * 128
                ]


def pack(qkv, labels, chunks):
    tok, heads, width = qkv.shape
    rows = chunks * (width // 128) * tok + 8
    whole = pl.BlockSpec(memory_space=pltpu.VMEM)
    return pl.pallas_call(
        functools.partial(pack_kernel, chunks=chunks),
        out_shape=jax.ShapeDtypeStruct((heads // chunks, rows, 128), jnp.bfloat16),
        in_specs=[whole, whole],
        out_specs=whole,
        compiler_params=pltpu.CompilerParams(vmem_limit_bytes=32 << 20),
        name="pack",
    )(qkv, labels)


def unpack_kernel(x_ref, o_ref):
    o_ref[...] = jnp.swapaxes(x_ref[...].astype(jnp.float32), 0, 1).astype(jnp.bfloat16)


def unpack(back):
    heads, tok, head_size = back.shape
    return pl.pallas_call(
        unpack_kernel,
        out_shape=jax.ShapeDtypeStruct((tok, heads, head_size), jnp.bfloat16),
        grid=(tok // STEP,),
        in_specs=[pl.BlockSpec((heads, STEP, head_size), lambda i: (0, i, 0))],
        out_specs=pl.BlockSpec((STEP, heads, head_size), lambda i: (i, 0, 0)),
        name="unpack",
    )(back)


def attend_kernel(lab_ref, x_ref, o_ref, v_ref, *, share, rate):
    nseq, _, head_size = x_ref.shape
    chunks = lab_ref.shape[0]
    rows = nseq * share
    ramp = lax.broadcasted_iota(jnp.int32, (QB, QB), 1) <= lax.broadcasted_iota(
        jnp.int32, (QB, QB), 0
    )

    def rows_of(chunk, part, first, count):
        base = (chunk * 3 + part) * share
        piece = x_ref[first // share : (first + count) // share, base : base + share, :]
        return piece.reshape(count, head_size)

    for chunk in range(chunks):
        v_ref[chunk, :, :head_size] = rows_of(chunk, 2, 0, rows)
        v_ref[chunk, :, head_size:] = jnp.ones((rows, 128), jnp.bfloat16)

    def score(chunk, block):
        return lax.dot_general(
            rows_of(chunk, 0, block * QB, QB),
            rows_of(chunk, 1, 0, (block + 1) * QB),
            (((1,), (1,)), ((), ())),
            preferred_element_type=jnp.float32,
        )

    def weigh(chunk, block, s):
        row0 = block * QB
        stop = row0 + QB
        lab_q = jnp.concatenate(
            [
                jnp.transpose(jnp.broadcast_to(lab_ref[chunk, i : i + 1, :], (128, 128)))
                for i in range(row0 // 128, stop // 128)
            ],
            axis=0,
        )
        pieces = []
        for i in range(stop // 128):
            keep = lab_q == lab_ref[chunk, i : i + 1, :]
            if i * 128 >= row0:
                keep = keep & ramp[:, i * 128 - row0 : i * 128 - row0 + 128]
            pieces.append(jnp.where(keep, s[:, i * 128 : (i + 1) * 128], NEG))
        peak = functools.reduce(jnp.maximum, pieces)
        peak = jnp.broadcast_to(jnp.max(peak, axis=1, keepdims=True), (QB, 128))
        pieces = [jnp.exp2((piece - peak) * rate).astype(jnp.bfloat16) for piece in pieces]
        return jnp.concatenate(pieces, axis=1)

    def blend(chunk, block, weights):
        row0 = block * QB
        stop = row0 + QB
        both = jnp.dot(weights, v_ref[chunk, :stop, :], preferred_element_type=jnp.float32)
        out = both[:, :head_size] / both[:, head_size:]
        o_ref[row0 // share : stop // share, chunk * share : (chunk + 1) * share] = out.astype(
            jnp.bfloat16
        ).reshape(QB // share, share, head_size)

    blocks = rows // QB
    tasks = [
        (chunk, step if chunk % 2 == 0 else blocks - 1 - step)
        for step in range(blocks)
        for chunk in range(chunks)
    ]
    ahead = score(*tasks[0])
    behind = None
    for place, task in enumerate(tasks):
        s = ahead
        if place + 1 < len(tasks):
            ahead = score(*tasks[place + 1])
        weights = weigh(*task, s)
        if behind is not None:
            blend(*behind)
        behind = (*task, weights)
    blend(*behind)


def attend(labels, x, chunks, share):
    nseq, _, head_size = x.shape
    rows = nseq * share
    rate = math.log2(math.e) / math.sqrt(head_size)
    whole = pl.BlockSpec(memory_space=pltpu.VMEM)
    return pl.pallas_call(
        functools.partial(attend_kernel, share=share, rate=rate),
        out_shape=jax.ShapeDtypeStruct((nseq, chunks * share, head_size), jnp.bfloat16),
        in_specs=[whole, whole],
        out_specs=whole,
        scratch_shapes=[pltpu.VMEM((chunks, rows, head_size + 128), jnp.bfloat16)],
        compiler_params=pltpu.CompilerParams(vmem_limit_bytes=40 << 20),
        name="attend",
    )(labels, x)


def cross_kernel(me_ref, x_ref, lab_ref, o_ref, buf_ref, labs_ref, out_ref, in_sems, out_sems):
    steps, count, heads, _ = buf_ref.shape
    nseq = o_ref.shape[0]
    half = nseq // 2
    tok = steps * count
    lane = pl.multiple_of(jnp.where(me_ref[0] >= half, 0, 128), 128)
    loads = [
        pltpu.make_async_copy(
            x_ref.at[pl.ds(step * count, count), :, pl.ds(lane, 256)],
            buf_ref.at[step],
            in_sems.at[step],
        )
        for step in range(steps)
    ]
    loads.append(pltpu.make_async_copy(lab_ref, labs_ref, in_sems.at[steps]))
    for load in loads:
        load.start()
    stores = []

    def store(row, rows):
        piece = (slice(None), pl.ds(row, rows), slice(None))
        stores.append(
            pltpu.make_async_copy(out_ref.at[piece], o_ref.at[piece], out_sems.at[len(stores)])
        )
        stores[-1].start()

    for step in range(steps):
        loads[step].wait()
        turned = jnp.swapaxes(buf_ref[step].astype(jnp.float32), 0, 1).astype(jnp.bfloat16)
        for part in range(4):
            row = part * tok + step * count
            lanes = slice(part // 2 * 128, part // 2 * 128 + 128)
            for dst in range(nseq):
                out_ref[dst, row : row + count, :] = turned[2 * dst + part % 2, :, lanes]
            store(row, count)
    loads[steps].wait()
    pad = jnp.zeros((4, 128), jnp.float32)
    for dst in range(nseq):
        other = dst ^ half
        labels = [labs_ref[2 * dst : 2 * dst + 2, :], labs_ref[2 * other : 2 * other + 2, :]]
        labels = [piece.astype(jnp.float32) for piece in labels]
        out_ref[dst, 4 * tok : 4 * tok + 8, :] = jnp.concatenate(labels + [pad], axis=0).astype(
            jnp.bfloat16
        )
    store(4 * tok, 8)
    for copy in stores:
        copy.wait()


def near_kernel(me_ref, x_ref, *rest):
    near_refs, turn_ref = rest[:-1], rest[-1]
    tok, heads, width = x_ref.shape
    half = len(near_refs)
    me = me_ref[0]
    for first in range(0, tok, 32):
        piece = x_ref[first : first + 32].astype(jnp.float32)
        turned = jnp.swapaxes(piece, 0, 1).astype(jnp.bfloat16)
        for head in range(heads):
            for part in range(3):
                turn_ref[head, part, first : first + 32, :] = turned[
                    head, :, part * 128 : (part + 1) * 128
                ]
    near_part = jnp.where(me >= half, 2, 0)
    for k, near_ref in enumerate(near_refs):
        dst = me ^ k
        other = dst ^ half
        for j in range(2):
            near_ref[j * tok : (j + 1) * tok, :] = turn_ref[2 * dst + j, near_part]
            for part in range(3):
                row = (2 + 2 * part + j) * tok
                near_ref[row : row + tok, :] = turn_ref[2 * other + j, part]


def spread(me, qkv, labels, nseq):
    tok, heads, width = qkv.shape
    whole = pl.BlockSpec(memory_space=pltpu.VMEM)
    scalar = pl.BlockSpec(memory_space=pltpu.SMEM)
    hbm = pl.BlockSpec(memory_space=pl.ANY)
    params = pltpu.CompilerParams(vmem_limit_bytes=12 << 20)
    cross = pl.pallas_call(
        cross_kernel,
        out_shape=jax.ShapeDtypeStruct((nseq, 4 * tok + 8, 128), jnp.bfloat16),
        in_specs=[scalar, hbm, hbm],
        out_specs=hbm,
        scratch_shapes=[
            pltpu.VMEM((4, tok // 4, heads, 256), jnp.bfloat16),
            pltpu.VMEM(labels.shape, labels.dtype),
            pltpu.VMEM((nseq, 4 * tok + 8, 128), jnp.bfloat16),
            pltpu.SemaphoreType.DMA((5,)),
            pltpu.SemaphoreType.DMA((17,)),
        ],
        compiler_params=pltpu.CompilerParams(vmem_limit_bytes=58 << 20),
        name="cross",
    )(me, qkv, labels)
    near = pl.pallas_call(
        near_kernel,
        out_shape=[jax.ShapeDtypeStruct((8 * tok, 128), jnp.bfloat16)] * (nseq // 2),
        in_specs=[scalar, whole],
        out_specs=[whole] * (nseq // 2),
        scratch_shapes=[pltpu.VMEM((heads, 3, tok, 128), jnp.bfloat16)],
        compiler_params=params,
        name="near",
    )(me, qkv)
    return cross, near


def run_tasks(tasks, score, weigh, blend):
    ahead = score(*tasks[0])
    behind = None
    for place, task in enumerate(tasks):
        s = ahead
        if place + 1 < len(tasks):
            ahead = score(*tasks[place + 1])
        found = weigh(*task, s)
        if behind is not None:
            blend(*behind)
        behind = (*task, *found)
    blend(*behind)


def dot_t(a, b):
    return lax.dot_general(a, b, (((1,), (1,)), ((), ())), preferred_element_type=jnp.float32)


def soften(s, lab_q, lab_k, diagonal, rate):
    pieces = []
    for i, lab in enumerate(lab_k):
        keep = lab_q == lab
        if diagonal is not None and i * 128 >= diagonal:
            lanes = lax.broadcasted_iota(jnp.int32, (QB, 128), 1) + (i * 128 - diagonal)
            keep = keep & (lanes <= lax.broadcasted_iota(jnp.int32, (QB, 128), 0))
        pieces.append(jnp.where(keep, s[:, i * 128 : (i + 1) * 128], NEG))
    peak = functools.reduce(jnp.maximum, pieces)
    peak = jnp.broadcast_to(jnp.max(peak, axis=1, keepdims=True), (QB, 128))
    pieces = [jnp.exp2((piece - peak) * rate).astype(jnp.bfloat16) for piece in pieces]
    return jnp.concatenate(pieces, axis=1), peak


def columns(rows):
    return jnp.concatenate(
        [jnp.transpose(jnp.broadcast_to(row, (128, 128))) for row in rows], axis=0
    )


def three_parts(stats):
    rows = []
    for row in stats:
        for _ in range(3):
            part = row.astype(jnp.bfloat16).astype(jnp.float32)
            rows.append(part)
            row = row - part
    rows.append(jnp.zeros((8 - len(rows), 128), jnp.float32))
    return jnp.concatenate(rows, axis=0).astype(jnp.bfloat16)


def finish(both, peak, rate, tok):
    num, total = both[:, :128], both[:, 128:]
    lse = peak * rate + jnp.log2(total)
    rows = [jnp.transpose(lse[i : i + tok, :])[:1, :] for i in range(0, QB, tok)]
    return num / total, rows


def far_kernel(me_ref, lab_ref, x_ref, o_ref, stat_ref, half_ref, v_ref, *, tok, rate):
    nseq = x_ref.shape[0]
    half = nseq // 2
    span = half * tok
    per = QB // tok
    for j in range(2):
        v_ref[j, :, :128] = x_ref[:half, (2 + j) * tok : (3 + j) * tok, :].reshape(span, 128)
        v_ref[j, :, 128:] = jnp.ones((span, 128), jnp.bfloat16)

    def score(j, block):
        first = half + block * per
        q = x_ref[first : first + per, j * tok : (j + 1) * tok, :].reshape(QB, 128)
        return dot_t(q, x_ref[:half, j * tok : (j + 1) * tok, :].reshape(span, 128))

    def weigh(j, block, s):
        first = half + block * per
        lab_q = columns([lab_ref[j, first + i : first + i + 1, :] for i in range(per)])
        return soften(s, lab_q, [lab_ref[j, i : i + 1, :] for i in range(half)], None, rate)

    def blend(j, block, weights, peak):
        both = jnp.dot(weights, v_ref[j], preferred_element_type=jnp.float32)
        out, rows = finish(both, peak, rate, tok)
        for i, row in enumerate(rows):
            stat_ref[j, block * per + i : block * per + i + 1, :] = row
        o_ref[j, block * QB : (block + 1) * QB, :] = out

    run_tasks([(j, block) for block in range(span // QB) for j in range(2)], score, weigh, blend)
    first = jnp.where(me_ref[0] >= half, half, 0)
    for kind in range(4):
        half_ref[kind] = x_ref[pl.ds(first, half), kind * tok : (kind + 1) * tok, :].reshape(
            span, 128
        )


def far_of(me, labels, x, tok, rate):
    half = x.shape[0] // 2
    whole = pl.BlockSpec(memory_space=pltpu.VMEM)
    return pl.pallas_call(
        functools.partial(far_kernel, tok=tok, rate=rate),
        out_shape=[
            jax.ShapeDtypeStruct((2, half * tok, 128), jnp.float32),
            jax.ShapeDtypeStruct((2, half, 128), jnp.float32),
            jax.ShapeDtypeStruct((4, half * tok, 128), jnp.bfloat16),
        ],
        in_specs=[pl.BlockSpec(memory_space=pltpu.SMEM), whole, whole],
        out_specs=[whole, whole, whole],
        scratch_shapes=[pltpu.VMEM((2, half * tok, 256), jnp.bfloat16)],
        compiler_params=pltpu.CompilerParams(vmem_limit_bytes=16 << 20),
        name="far",
    )(me, labels, x)


def own_kernel(me_ref, lab_ref, far_ref, far_stat_ref, half_ref, *rest, tok, rate):
    half = far_stat_ref.shape[1]
    near_refs, o_ref = rest[:half], rest[half]
    q_ref, v_ref, out_ref, sems = rest[half + 1 :]
    span = half * tok
    per = QB // tok
    me = me_ref[0]
    upper = me >= half
    up = upper.astype(jnp.int32)
    stores = []

    def store(first, count, row, rows):
        piece = (pl.ds(first, count), pl.ds(row, rows), slice(None))
        stores.append(
            pltpu.make_async_copy(out_ref.at[piece], o_ref.at[piece], sems.at[len(stores)])
        )
        stores[-1].start()

    for j in range(2):
        out_ref[pl.ds((1 - up) * half, half), j * tok : (j + 1) * tok, :] = (
            far_ref[j].astype(jnp.bfloat16).reshape(half, tok, 128)
        )
    for i in range(half):
        stats = three_parts([far_stat_ref[j, i : i + 1, :] for j in range(2)])
        out_ref[(1 - up) * half + i, 2 * tok : 2 * tok + 8, :] = stats
        out_ref[up * half + i, 2 * tok : 2 * tok + 8, :] = jnp.zeros((8, 128), jnp.bfloat16)
    store((1 - up) * half, half, 0, 2 * tok + 8)
    store(up * half, half, 2 * tok, 8)
    places = [pl.ds(pl.multiple_of(((me ^ k) % half) * tok, tok), tok) for k in range(half)]

    @pl.when(upper)
    def _():
        for j in range(2):
            q_ref[j] = half_ref[j]
            for place, near_ref in zip(places, near_refs):
                v_ref[j, place, :128] = near_ref[j * tok : (j + 1) * tok, :]

    @pl.when(jnp.logical_not(upper))
    def _():
        for j in range(2):
            v_ref[j, :, :128] = half_ref[2 + j]
            for place, near_ref in zip(places, near_refs):
                q_ref[j, place, :] = near_ref[j * tok : (j + 1) * tok, :]

    for j in range(2):
        v_ref[j, :, 128:] = jnp.ones((span, 128), jnp.bfloat16)

    def lab_of(j, first, count):
        return [lab_ref[j, pl.ds(up * half + first + i, 1), :] for i in range(count)]

    def score(j, block):
        k = half_ref[2 * up + j, : (block + 1) * QB, :]
        return dot_t(q_ref[j, block * QB : (block + 1) * QB, :], k)

    def weigh(j, block, s):
        lab_q = columns(lab_of(j, block * per, per))
        return soften(s, lab_q, lab_of(j, 0, (block + 1) * per), block * QB, rate)

    def blend(j, block, weights, peak):
        both = jnp.dot(
            weights, v_ref[j, : (block + 1) * QB, :], preferred_element_type=jnp.float32
        )
        total = both[:, 128:]
        near = both[:, :128] / total
        rows = [
            far_stat_ref[j, i : i + 1, :] for i in range(block * per, (block + 1) * per)
        ]
        gap = peak * rate + jnp.log2(total) - columns(rows)
        weight = jnp.where(upper, 1.0 / (1.0 + jnp.exp2(gap)), 0.0)
        far = far_ref[j, block * QB : (block + 1) * QB, :]
        out = near + (far - near) * weight
        out_ref[pl.ds(up * half + block * per, per), j * tok : (j + 1) * tok, :] = out.astype(
            jnp.bfloat16
        ).reshape(per, tok, 128)
        store(up * half + block * per, per, j * tok, tok)

    blocks = span // QB
    tasks = [
        (j, block if j == 0 else blocks - 1 - block) for block in range(blocks) for j in range(2)
    ]
    run_tasks(tasks, score, weigh, blend)
    for copy in stores:
        copy.wait()


def own(me, labels, far, near, tok, rate):
    half = len(near)
    nseq = 2 * half
    span = half * tok
    whole = pl.BlockSpec(memory_space=pltpu.VMEM)
    return pl.pallas_call(
        functools.partial(own_kernel, tok=tok, rate=rate),
        out_shape=jax.ShapeDtypeStruct((nseq, 2 * tok + 8, 128), jnp.bfloat16),
        in_specs=[pl.BlockSpec(memory_space=pltpu.SMEM)] + [whole] * (4 + half),
        out_specs=pl.BlockSpec(memory_space=pl.ANY),
        scratch_shapes=[
            pltpu.VMEM((2, span, 128), jnp.bfloat16),
            pltpu.VMEM((2, span, 256), jnp.bfloat16),
            pltpu.VMEM((nseq, 2 * tok + 8, 128), jnp.bfloat16),
            pltpu.SemaphoreType.DMA((2 + 2 * span // QB,)),
        ],
        compiler_params=pltpu.CompilerParams(vmem_limit_bytes=16 << 20),
        name="own",
    )(me, labels, *far, *near)


def partner_kernel(me_ref, lab_ref, *rest, tok, rate):
    half = (len(rest) - 5) // 2
    near_refs, o_refs = rest[:half], rest[half : 2 * half]
    q_ref, k_ref, v_ref, out_ref, stat_ref = rest[2 * half :]
    span = half * tok
    me = me_ref[0]
    up = (me >= half).astype(jnp.int32)
    for j in range(2):
        v_ref[j, :, 128:] = jnp.ones((span, 128), jnp.bfloat16)
        for k, near_ref in enumerate(near_refs):
            place = pl.ds(pl.multiple_of(((me ^ k) % half) * tok, tok), tok)
            q_ref[j, place, :] = near_ref[(2 + j) * tok : (3 + j) * tok, :]
            k_ref[j, place, :] = near_ref[(4 + j) * tok : (5 + j) * tok, :]
            v_ref[j, place, :128] = near_ref[(6 + j) * tok : (7 + j) * tok, :]

    def lab_of(j, first, count):
        return [lab_ref[2 + j, pl.ds(up * half + first + i, 1), :] for i in range(count)]

    per = QB // tok

    def score(j, block):
        return dot_t(q_ref[j, pl.ds(block * QB, QB), :], k_ref[j, : (block + 1) * QB, :])

    def weigh(j, block, s):
        lab_q = columns(lab_of(j, block * per, per))
        return soften(s, lab_q, lab_of(j, 0, (block + 1) * per), block * QB, rate)

    def blend(j, block, weights, peak):
        both = jnp.dot(
            weights, v_ref[j, : (block + 1) * QB, :], preferred_element_type=jnp.float32
        )
        num, total = both[:, :128], both[:, 128:]
        lse = peak * rate + jnp.log2(total)
        out = (num / total).astype(jnp.bfloat16)
        for i in range(per):
            turned = jnp.transpose(lse[i * tok : (i + 1) * tok, :])
            stat_ref[j, block * per + i : block * per + i + 1, :] = turned[:1, :]
            out_ref[block * per + i, j * tok : (j + 1) * tok, :] = out[i * tok : (i + 1) * tok, :]

    blocks = span // QB
    tasks = [
        (j, block if j == 0 else blocks - 1 - block) for block in range(blocks) for j in range(2)
    ]
    run_tasks(tasks, score, weigh, blend)
    for i in range(half):
        stats = three_parts([stat_ref[j, i : i + 1, :] for j in range(2)])
        out_ref[i, 2 * tok : 2 * tok + 8, :] = stats
    for k, o_ref in enumerate(o_refs):
        o_ref[...] = out_ref[(me ^ k) % half]


def partner(me, labels, near, tok, rate):
    half = len(near)
    span = half * tok
    whole = pl.BlockSpec(memory_space=pltpu.VMEM)
    return pl.pallas_call(
        functools.partial(partner_kernel, tok=tok, rate=rate),
        out_shape=[jax.ShapeDtypeStruct((2 * tok + 8, 128), jnp.bfloat16)] * half,
        in_specs=[pl.BlockSpec(memory_space=pltpu.SMEM)] + [whole] * (1 + half),
        out_specs=[whole] * half,
        scratch_shapes=[
            pltpu.VMEM((2, span, 128), jnp.bfloat16),
            pltpu.VMEM((2, span, 128), jnp.bfloat16),
            pltpu.VMEM((2, span, 256), jnp.bfloat16),
            pltpu.VMEM((half, 2 * tok + 8, 128), jnp.bfloat16),
            pltpu.VMEM((2, half, 128), jnp.float32),
        ],
        compiler_params=pltpu.CompilerParams(vmem_limit_bytes=16 << 20),
        name="partner",
    )(me, labels, *near)


def merge_kernel(me_ref, x_ref, *rest, tok):
    nseq = x_ref.shape[0]
    half = nseq // 2
    near_refs, o_ref = rest[:half], rest[half]
    head_ref, out_ref, sems = rest[half + 1 :]
    me = me_ref[0]
    upper = me >= half
    up = upper.astype(jnp.int32)
    down = 1 - up
    heads = 2 * nseq
    for i in range(half):
        for j in range(2):
            head_ref[up * (heads // 2) + 2 * i + j] = x_ref[
                up * half + i, j * tok : (j + 1) * tok, :
            ].astype(jnp.float32)
    for k, near_ref in zip(HOPS, near_refs):
        place = (me ^ k) % half
        far_stats = x_ref[down * half + place, 2 * tok : 2 * tok + 8, :].astype(jnp.float32)
        near_stats = near_ref[2 * tok : 2 * tok + 8, :].astype(jnp.float32)
        for j in range(2):
            near_lse = sum(near_stats[3 * j + c : 3 * j + c + 1, :] for c in range(3))
            far_lse = sum(far_stats[3 * j + c : 3 * j + c + 1, :] for c in range(3))
            weight = jnp.where(upper, 1.0 / (1.0 + jnp.exp2(near_lse - far_lse)), 0.0)
            weight = jnp.transpose(jnp.broadcast_to(weight, (128, tok)))
            far = x_ref[down * half + place, j * tok : (j + 1) * tok, :].astype(jnp.float32)
            near = near_ref[j * tok : (j + 1) * tok, :].astype(jnp.float32)
            head_ref[down * (heads // 2) + 2 * place + j] = near + (far - near) * weight
    stores = []
    for first in range(0, tok, 32):
        piece = head_ref[:, first : first + 32, :]
        out_ref[first : first + 32] = jnp.swapaxes(piece, 0, 1).astype(jnp.bfloat16)
        stores.append(
            pltpu.make_async_copy(
                out_ref.at[pl.ds(first, 32)], o_ref.at[pl.ds(first, 32)], sems.at[len(stores)]
            )
        )
        stores[-1].start()
    for copy in stores:
        copy.wait()


def merge(me, x, near, tok):
    nseq = x.shape[0]
    whole = pl.BlockSpec(memory_space=pltpu.VMEM)
    return pl.pallas_call(
        functools.partial(merge_kernel, tok=tok),
        out_shape=jax.ShapeDtypeStruct((tok, 2 * nseq, 128), jnp.bfloat16),
        in_specs=[pl.BlockSpec(memory_space=pltpu.SMEM)] + [whole] * (1 + nseq // 2),
        out_specs=pl.BlockSpec(memory_space=pl.ANY),
        scratch_shapes=[
            pltpu.VMEM((2 * nseq, tok, 128), jnp.float32),
            pltpu.VMEM((tok, 2 * nseq, 128), jnp.bfloat16),
            pltpu.SemaphoreType.DMA((tok // 32,)),
        ],
        compiler_params=pltpu.CompilerParams(vmem_limit_bytes=12 << 20),
        name="merge",
    )(me, x, *near)


def two_halves(qkv, labels):
    tok, heads, width = qkv.shape
    nseq = lax.axis_size("seq")
    rate = math.log2(math.e) / math.sqrt(width // 3)
    me = lax.axis_index("seq").astype(jnp.int32).reshape(1)

    def exchange(x):
        return lax.all_to_all(x, "seq", split_axis=0, concat_axis=0, tiled=True)

    def swap(blocks):
        moved = list(blocks)
        for k in reversed(range(1, len(blocks))):
            moved[k] = lax.ppermute(blocks[k], "seq", [(i, i ^ k) for i in range(nseq)])
        return moved

    cross, near = spread(me, qkv, labels, nseq)
    near = swap(near)
    cross = exchange(cross)
    labels = jnp.transpose(cross[:, 4 * tok : 4 * tok + 4, :].astype(jnp.int32), (1, 0, 2))
    far = far_of(me, labels, cross, tok, rate)
    back = exchange(own(me, labels, far, near, tok, rate))
    near_back = swap(partner(me, labels, near, tok, rate))
    return merge(me, back, [near_back[k] for k in HOPS], tok)


def local(qkv, routes):
    tok, heads, width = qkv.shape
    head_size = width // 3
    nseq = lax.axis_size("seq")
    clusters = nseq * tok // CLEN
    pairs_dev = heads * tok // CLEN
    chunks = max(1, pairs_dev // clusters)
    split = max(1, clusters // pairs_dev)
    share = tok // split

    def exchange(x):
        return lax.all_to_all(x, "seq", split_axis=0, concat_axis=0, tiled=True)

    labels = jnp.transpose(routes)
    paired = nseq == 2 * len(HOPS) and nseq * tok // 2 % QB == 0
    if split == 1 and chunks == 2 and paired and tok == 128 and head_size == 128:
        return two_halves(qkv, labels)
    if split == 1:
        rows = exchange(pack(qkv, labels, chunks))
    else:
        group = labels // pairs_dev
        member = group[:, :, None] == jnp.arange(split, dtype=jnp.int32)[None, None, :]
        rank = jnp.cumsum(member.astype(jnp.int32), axis=1) - 1
        slot = group * share + jnp.sum(jnp.where(member, rank, 0), axis=2)
        pick = slot[:, None, :] == jnp.arange(tok, dtype=jnp.int32)[None, :, None]
        moved = jnp.einsum(
            "hst,thd->hsd", pick.astype(jnp.bfloat16), qkv, preferred_element_type=jnp.float32
        ).astype(jnp.bfloat16)
        labels = jnp.sum(jnp.where(pick, labels[:, None, :], 0), axis=2)
        moved = moved.reshape(nseq, share, 3, head_size)
        moved = jnp.transpose(moved, (0, 2, 1, 3)).reshape(nseq, 3 * share, head_size)
        extra = labels.reshape(nseq, 1, share).astype(jnp.bfloat16)
        extra = jnp.pad(extra, ((0, 0), (0, 7), (0, head_size - share)))
        rows = exchange(jnp.concatenate([moved, extra], axis=1))
    first = chunks * 3 * share
    arrived = rows[:, first : first + chunks, :share].astype(jnp.int32)
    arrived = jnp.transpose(arrived, (1, 0, 2)).reshape(chunks, nseq * share // 128, 128)
    back = exchange(attend(arrived, rows, chunks, share)).reshape(heads, tok, head_size)
    if split > 1:
        back = jnp.einsum(
            "hst,hsd->htd", pick.astype(jnp.bfloat16), back, preferred_element_type=jnp.float32
        ).astype(jnp.bfloat16)
    return unpack(back)


def solution(mesh):
    placed = (P(("groups", "seq"), None, None), P(("groups", "seq"), None))
    return jax.shard_map(
        local,
        mesh=mesh,
        in_specs=placed,
        out_specs=P(("groups", "seq"), None, None),
        check_vma=False,
    )
```
